32 devices in a mesh: depth: 4 (over x, core), rows: 8 (over z, y).
Axes of the slice: x: 2, y: 2, z: 4, core: 2. Of those that a mesh axis runs over, the one named last changes fastest.
Arguments:
- volume: bfloat16 [4, 64, 256, 4096], P(None, 'depth', 'rows')
- shear_rows: int32 [64], P('depth'), may hold values from -8 to 8, as said below
- shear_cols: int32 [64], P('depth'), may hold values from -8 to 8, as said below
- warp_cols: int32 [256], replicated, may hold values from -8 to 8, as said below
- warp_rows: int32 [4096], P('depth'), may hold values from -8 to 8, as said below
Outputs:
- final_image: float32 [4, 256, 4096], P(None, 'rows', 'depth')
The draws below stay inside these ranges and needn't reach their ends.
Inputs may be any that keep to these rules, and one draw needn't show every extreme that they name: `shear_rows`: both -8 and 8 occur. `shear_cols`: both -8 and 8 occur. `warp_cols`: both -8 and 8 occur. `warp_rows`: both -8 and 8 occur.
All inputs are finite; a program needn't handle non-finite values.
Results may differ from the reference program's by a relative error of at most 0.0017.
Values may be sent and summed in bfloat16 or wider, within the bound.
A program may use at most 192 MiB of HBM per device.

```python
import jax
import jax.numpy as jnp
from jax import lax

X = 4096
SHIFT = 8
Z = 64
Y = 256


def draw_offsets(key, count):
    first_key, second_key, third_key = jax.random.split(key, 3)
    values = jax.random.randint(first_key, (count,), -SHIFT, SHIFT + 1)
    high_spot = jax.random.randint(second_key, (), 0, count)
    low_spot = (high_spot + 1 + jax.random.randint(third_key, (), 0, count - 1)) % count
    values = values.at[high_spot].set(SHIFT)
    values = values.at[low_spot].set(-SHIFT)
    return values.astype(jnp.int32)


def draw_volume(key, part):
    colour_key, opacity_key = jax.random.split(jax.random.fold_in(key, 11))
    colour = jax.random.uniform(colour_key, (3, Z, Y, X), jnp.float32, 0.0, 2.0)
    opacity = jnp.exp(jax.random.uniform(opacity_key, (1, Z, Y, X), jnp.float32, jnp.log(0.001), jnp.log(0.06)))
    return jnp.concatenate([colour, opacity], 0).astype(jnp.bfloat16)


def draw_shear_rows(key, part):
    return draw_offsets(jax.random.fold_in(key, 21), Z)


def draw_shear_cols(key, part):
    return draw_offsets(jax.random.fold_in(key, 22), Z)


def draw_warp_cols(key, part):
    return draw_offsets(jax.random.fold_in(key, 23), Y)


def draw_warp_rows(key, part):
    return draw_offsets(jax.random.fold_in(key, 24), X)


def setup_inputs(seed: int = 0) -> dict:
    arg_keys = jax.random.split(jax.random.key(seed), 6)
    volume = draw_volume(jax.random.fold_in(arg_keys[5], 71), 0)
    shear_rows = draw_shear_rows(jax.random.fold_in(arg_keys[5], 71), 0)
    shear_cols = draw_shear_cols(jax.random.fold_in(arg_keys[5], 71), 0)
    warp_cols = draw_warp_cols(jax.random.fold_in(arg_keys[5], 71), 0)
    warp_rows = draw_warp_rows(jax.random.fold_in(arg_keys[5], 71), 0)
    return {"volume": volume, "shear_rows": shear_rows, "shear_cols": shear_cols, "warp_cols": warp_cols, "warp_rows": warp_rows}


def weight_of(offset):
    return jnp.where(offset == 0, 0.5, jnp.where(jnp.abs(offset) == 1, 0.25, 0.0)).astype(jnp.float32)


def over_front(front_part, back_part):
    return front_part + (1.0 - front_part[3:4]) * back_part


def premultiply(slab):
    opacity = slab[3:4]
    return jnp.concatenate([slab[:3] * opacity, opacity], 0)


def shear_slice(extended, row_shift, col_shift, band_rows, band_cols, rim_width):
    band_sum = jnp.zeros((4, band_rows, band_cols + 2 * rim_width), jnp.float32)
    for offset, factor in ((-1, 0.25), (0, 0.5), (1, 0.25)):
        start = (rim_width + row_shift + offset).astype(jnp.int32)
        band_sum = band_sum + factor * lax.dynamic_slice_in_dim(extended, start, band_rows, 1)
    sheared = jnp.zeros((4, band_rows, band_cols), jnp.float32)
    for offset, factor in ((-1, 0.25), (0, 0.5), (1, 0.25)):
        start = (rim_width + col_shift + offset).astype(jnp.int32)
        sheared = sheared + factor * lax.dynamic_slice_in_dim(band_sum, start, band_cols, 2)
    return sheared


def shift_columns(picture, shifts, band_cols, rim_width):
    result = jnp.zeros((4, picture.shape[1], band_cols), jnp.float32)
    for offset in range(-rim_width, rim_width + 1):
        kernel_col = weight_of(offset - shifts)[None, :, None]
        result = result + kernel_col * picture[:, :, rim_width + offset:rim_width + offset + band_cols]
    return result


def shift_rows(picture, shifts, band_rows, rim_width):
    result = jnp.zeros((4, band_rows, picture.shape[2]), jnp.float32)
    for offset in range(-rim_width, rim_width + 1):
        kernel_row = weight_of(offset - shifts)[None, None, :]
        result = result + kernel_row * picture[:, rim_width + offset:rim_width + offset + band_rows, :]
    return result


def reference(volume, shear_rows, shear_cols, warp_cols, warp_rows):
    rim_width = SHIFT + 1
    slices_first = jnp.moveaxis(volume, 1, 0)

    def add_slice(accumulated, pieces_in):
        slice_now, row_shift, col_shift = pieces_in
        extended = jnp.pad(premultiply(slice_now.astype(jnp.float32)), ((0, 0), (rim_width, rim_width), (rim_width, rim_width)))
        return over_front(accumulated, shear_slice(extended, row_shift, col_shift, Y, X, rim_width)), None

    start_image = jnp.zeros((4, Y, X), jnp.float32)
    intermediate, _ = lax.scan(add_slice, start_image, (slices_first, shear_rows, shear_cols))
    padded_cols = jnp.pad(intermediate, ((0, 0), (0, 0), (rim_width, rim_width)))
    across = shift_columns(padded_cols, warp_cols, X, rim_width)
    padded_rows = jnp.pad(across, ((0, 0), (rim_width, rim_width), (0, 0)))
    return shift_rows(padded_rows, warp_rows, Y, rim_width)
```

```python
import functools

import jax
import jax.numpy as jnp
from jax import lax
from jax.experimental import pallas as pl
from jax.experimental.pallas import tpu as pltpu
from jax.sharding import PartitionSpec as P

SHIFT = 8
RIM = SHIFT + 1
GROUP = 8
EDGE = 16
LANES = 128
LEAD = 16
CHUNK = 512
BF = jnp.bfloat16
F32 = jnp.float32
MESH = pl.DeviceIdType.MESH


def weight_of(offset):
    return jnp.where(offset == 0, 0.5, jnp.where(jnp.abs(offset) == 1, 0.25, 0.0)).astype(F32)


def iota(shape, dim):
    return lax.broadcasted_iota(jnp.int32, shape, dim)


def groups_of(s, ou, od, total):
    gu = jnp.minimum(ou // GROUP, total - jnp.where(s > 0, 2, 1))
    gd = jnp.minimum(od // GROUP, total - jnp.where(s < 0, 2, 1))
    g0 = jnp.where(s >= 0, gu, total + gd)
    g1 = jnp.where(s > 0, gu + 1, total + gd + jnp.where(s < 0, 1, 0))
    return gu, gd, g0, g1


def slab_kernel(
    sizes, row_s, col_s, off_up, off_dn, at_up_ref, at_dn_ref, warp_ref, vol_hbm,
    mid_ref, low_ref, high_ref,
    vol, send_up, send_dn, recv_up, recv_dn, work, w_row, w_col, band, acc, outb, parts, wide_ref,
    load_sem, s_up, r_up, s_dn, r_dn, s_part, r_part,
):
    depth, n_rows = sizes
    chunks, channels, slab, rows, _ = vol.shape
    groups = send_up.shape[1]
    high = groups * GROUP
    cols = chunks * CHUNK
    tile = cols // depth
    per = CHUNK // LANES
    per_tile = tile // LANES
    pieces = tile // CHUNK
    flat = channels * rows
    me = lax.axis_index("depth")
    row = lax.axis_index("rows")
    has_up = row < n_rows - 1
    has_dn = row > 0
    above = jnp.maximum(row - 1, 0)
    below = jnp.minimum(row + 1, n_rows - 1)

    def load(i):
        return pltpu.make_async_copy(
            vol_hbm.at[:, :, :, pl.ds(pl.multiple_of(i * CHUNK, CHUNK), CHUNK)], vol.at[i], load_sem.at[i]
        )

    for i in range(chunks):
        load(i).start()

    barrier = pltpu.get_barrier_semaphore()
    for r in (lax.rem(row + 1, n_rows), lax.rem(row + n_rows - 1, n_rows)):
        pl.semaphore_signal(barrier, inc=1, device_id=(me, r), device_id_type=MESH)
    for m in range(1, depth):
        pl.semaphore_signal(barrier, inc=1, device_id=(lax.rem(me + m, depth), row), device_id_type=MESH)
    pl.semaphore_wait(barrier, depth + 1)

    def up_copy(i):
        return pltpu.make_async_remote_copy(
            send_up.at[i], recv_up.at[i], s_up.at[i], r_up.at[i], device_id=(me, above), device_id_type=MESH
        )

    def dn_copy(i):
        return pltpu.make_async_remote_copy(
            send_dn.at[i], recv_dn.at[i], s_dn.at[i], r_dn.at[i], device_id=(me, below), device_id_type=MESH
        )

    def send(i):
        @pl.when(has_dn)
        def _():
            up_copy(i).start()

        @pl.when(has_up)
        def _():
            dn_copy(i).start()

    @pl.loop(0, chunks)
    def _(i):
        load(i).wait()
        for at_ref, out, first in ((at_up_ref, send_up, 0), (at_dn_ref, send_dn, rows - EDGE)):
            pick = (iota((high, slab * EDGE), 0) == at_ref[...]).astype(F32).astype(BF)
            got = []
            for c in range(channels):
                source = vol[i, c, :, first : first + EDGE, :].reshape(slab * EDGE, CHUNK)
                got.append(jnp.dot(pick, source, preferred_element_type=F32))
            got = [g * got[-1] for g in got[:-1]] + [got[-1]]
            for g in range(groups):
                piece = [v[g * GROUP : (g + 1) * GROUP] for v in got]
                out[i, g] = jnp.concatenate(piece, 0).astype(BF)

        @pl.when(i > 0)
        def _():
            send(i - 1)

    send(chunks - 1)

    work[...] = jnp.zeros_like(work)
    band[...] = jnp.zeros_like(band)

    @pl.loop(0, slab)
    def _(k):
        s = row_s[k]
        ou = off_up[k]
        od = off_dn[k]
        gu, gd, _, _ = groups_of(s, ou, od, groups)
        count = jnp.maximum(0, 1 - s)
        row_up = rows + gu * GROUP - ou
        row_dn = gd * GROUP - od - count
        m = iota((flat, flat), 0)
        j = iota((flat, flat), 1)
        same = (m // rows) == (j // rows)
        w_row[k, :, :flat] = jnp.where(same, weight_of((j % rows) - (m % rows) - s), 0.0).astype(BF)
        wide = 2 * channels * GROUP
        m = iota((flat, wide), 0)
        j = iota((flat, wide), 1)
        second = j >= channels * GROUP
        q = j % GROUP
        same = (m // rows) == ((j // GROUP) % channels)
        first_row = jnp.where(s >= 0, row_up, row_dn)
        second_row = jnp.where(s > 0, row_up + GROUP, row_dn + jnp.where(s < 0, GROUP, 0))
        r = q + jnp.where(second, second_row, first_row)
        room = jnp.where(second, jnp.where(s > 0, r - rows, -1 - r), jnp.where(s >= 0, r - rows, -1 - r))
        kept = same & (room >= 0)
        w_row[k, :, flat : flat + wide] = jnp.where(kept, weight_of(r - (m % rows) - s), 0.0).astype(BF)
        shape = (2 * LANES, LANES)
        offset = iota(shape, 0) - iota(shape, 1) - (LANES - LEAD) - col_s[k]
        w_col[k] = weight_of(offset).astype(BF)

    def part_copy(i, w, count, owner, at, piece):
        return pltpu.make_async_remote_copy(
            outb.at[pl.ds(i * per + w, count)],
            parts.at[me, pl.ds(at, count)],
            s_part.at[i, piece],
            r_part.at[me, pieces if piece else lax.rem(i, pieces)],
            device_id=(owner, row),
            device_id_type=MESH,
        )

    def deliver(i, act, keep):
        owner = i // pieces
        at = lax.rem(i, pieces) * per

        @pl.when(owner != me)
        def _():
            act(part_copy(i, 0, per, owner, at, 0))

        if keep:
            @pl.when(owner == me)
            def _():
                parts[me, pl.ds(at, per)] = outb[pl.ds(i * per, per)]

        margin = (lax.rem(i, pieces) == 0) & (i > 0)
        left = jnp.maximum(owner - 1, 0)

        @pl.when(margin & (left != me))
        def _():
            act(part_copy(i, 0, 1, left, per_tile, 1))

        if keep:
            @pl.when(margin & (left == me))
            def _():
                parts[me, per_tile] = outb[i * per]

    def over(w, sheared):
        clear = 1.0 - acc[w, flat - rows :, :]
        for c in range(channels):
            acc[w, c * rows : (c + 1) * rows, :] += clear * sheared[c * rows : (c + 1) * rows]

    def store(i, w, at):
        x = i * CHUNK + w * LANES - LEAD + iota((flat, LANES), 1)
        outb[at] = jnp.where((x >= 0) & (x < cols), acc[w], 0.0).astype(BF)

    @pl.loop(0, chunks)
    def _(i):
        @pl.when(has_up)
        def _():
            up_copy(i).wait_recv()
            work[:groups] = recv_up[i]

        @pl.when(has_dn)
        def _():
            dn_copy(i).wait_recv()
            work[groups:] = recv_dn[i]

        acc[...] = jnp.zeros_like(acc)

        @pl.loop(0, slab)
        def _(k):
            _, _, g0, g1 = groups_of(row_s[k], off_up[k], off_dn[k], groups)
            band[k, :, :LANES] = band[k, :, CHUNK:]
            opacity = vol[i, channels - 1, k]
            own = [vol[i, c, k] * opacity for c in range(channels - 1)] + [opacity]
            data = jnp.concatenate(own + [work[g0], work[g1]], 0)
            weights = w_row[k, :, : flat + 2 * channels * GROUP]
            new = jnp.dot(weights, data, preferred_element_type=F32).astype(BF)
            band[k, :, LANES:] = new
            stack = [band[k, :, w * LANES : (w + 2) * LANES] for w in range(per)]
            sheared = jnp.dot(jnp.concatenate(stack, 0), w_col[k], preferred_element_type=F32)
            for w in range(per):
                over(w, sheared[w * flat : (w + 1) * flat])

        for w in range(per):
            store(i, w, i * per + w)

        @pl.when(i > 0)
        def _():
            deliver(i - 1, lambda copy: copy.start(), True)

    deliver(jnp.int32(chunks - 1), lambda copy: copy.start(), True)

    acc[0] = jnp.zeros_like(acc[0])

    @pl.loop(0, slab)
    def _(k):
        sheared = jnp.dot(band[k, :, CHUNK:], w_col[k, :LANES], preferred_element_type=F32)
        over(0, sheared)

    store(chunks, 0, chunks * per)

    def tail_copy():
        return pltpu.make_async_remote_copy(
            outb.at[pl.ds(chunks * per, 1)],
            parts.at[me, pl.ds(per_tile, 1)],
            s_part.at[chunks, 1],
            r_part.at[me, pieces],
            device_id=(jnp.int32(depth - 1), row),
            device_id_type=MESH,
        )

    @pl.when(me != depth - 1)
    def _():
        tail_copy().start()

    @pl.when(me == depth - 1)
    def _():
        parts[me, per_tile] = outb[chunks * per]

    for d in range(depth):
        @pl.when(me != d)
        def _():
            for p in range(pieces + 1):
                count = per if p < pieces else 1
                pltpu.make_async_remote_copy(
                    outb.at[pl.ds(0, count)],
                    parts.at[d, pl.ds(p * per, count)],
                    s_part.at[0, 0],
                    r_part.at[d, p],
                    device_id=(me, row),
                    device_id_type=MESH,
                ).wait_recv()

    for w in range(per_tile + 1):
        image = parts[0, w].astype(F32)
        image = image.reshape(channels, rows, LANES)
        for d in range(1, depth):
            back = parts[d, w].astype(F32).reshape(channels, rows, LANES)
            image = image + (1.0 - image[channels - 1 :]) * back
        wide_ref[:, w * LANES : (w + 1) * LANES] = image.reshape(flat, LANES)

    width = wide_ref.shape[1]
    amount = warp_ref[...] + SHIFT
    for c in range(channels):
        line = wide_ref[c * rows : (c + 1) * rows]
        line = 0.5 * line + 0.25 * (pltpu.roll(line, 1, 1) + pltpu.roll(line, width - 1, 1))
        line = pltpu.roll(line, width - (LEAD - SHIFT), 1)
        for bit in (1, 2, 4, 8, 16):
            line = jnp.where((amount & bit) != 0, pltpu.roll(line, width - bit, 1), line)
        across = line[:, :tile]
        mid_ref[c] = across
        low_ref[c] = across[:EDGE].astype(BF)
        high_ref[c] = across[rows - EDGE :].astype(BF)

    @pl.loop(0, chunks)
    def _(i):
        @pl.when(has_dn)
        def _():
            up_copy(i).wait_send()

        @pl.when(has_up)
        def _():
            dn_copy(i).wait_send()

        deliver(i, lambda copy: copy.wait_send(), False)

    @pl.when(me != depth - 1)
    def _():
        tail_copy().wait_send()


def slab_stage(high, number, depth, n_rows, volume, scalars, at_up, at_dn, warp):
    channels, slab, rows, cols = volume.shape
    chunks = cols // CHUNK
    groups = high // GROUP
    per = CHUNK // LANES
    tile = cols // depth
    flat = channels * rows
    pieces = tile // CHUNK
    smem = pl.BlockSpec(memory_space=pltpu.SMEM)
    vmem = pl.BlockSpec(memory_space=pltpu.VMEM)
    halo = pltpu.VMEM((chunks, groups, channels * GROUP, CHUNK), BF)
    half = jax.ShapeDtypeStruct((channels, EDGE, tile), BF)
    dma = pltpu.SemaphoreType.DMA
    return pl.pallas_call(
        functools.partial(slab_kernel, (depth, n_rows)),
        in_specs=[smem] * 4 + [vmem] * 3 + [pl.BlockSpec(memory_space=pl.ANY)],
        out_specs=[vmem] * 3,
        out_shape=[jax.ShapeDtypeStruct((channels, rows, tile), F32), half, half],
        scratch_shapes=[
            pltpu.VMEM((chunks, channels, slab, rows, CHUNK), BF),
            halo,
            halo,
            halo,
            halo,
            pltpu.VMEM((2 * groups, channels * GROUP, CHUNK), BF),
            pltpu.VMEM((slab, flat, 2 * LANES), BF),
            pltpu.VMEM((slab, 2 * LANES, LANES), BF),
            pltpu.VMEM((slab, flat, LANES + CHUNK), BF),
            pltpu.VMEM((per, flat, LANES), F32),
            pltpu.VMEM((chunks * per + 1, flat, LANES), BF),
            pltpu.VMEM((depth, tile // LANES + 1, flat, LANES), BF),
            pltpu.VMEM((flat, tile + LANES), F32),
            dma((chunks,)),
            dma((chunks,)),
            dma((chunks,)),
            dma((chunks,)),
            dma((chunks,)),
            dma((chunks + 1, 2)),
            dma((depth, pieces + 1)),
        ],
        compiler_params=pltpu.CompilerParams(
            collective_id=number, has_side_effects=True, vmem_limit_bytes=60 * 2**20
        ),
        name=f"slab_{high}",
    )(*scalars, at_up, at_dn, warp, volume)


def final_kernel(shift_ref, mid_ref, low_ref, high_ref, out_ref, ext_ref):
    channels, rows, tile = mid_ref.shape
    shifts = shift_ref[...]
    for c in range(channels):
        ext_ref[:EDGE] = low_ref[c].astype(F32)
        ext_ref[EDGE : EDGE + rows] = mid_ref[c]
        ext_ref[EDGE + rows :] = high_ref[c].astype(F32)
        moved = jnp.zeros((rows + 2, tile), F32)
        for v in range(-SHIFT, SHIFT + 1):
            start = EDGE + v - 1
            moved = jnp.where(shifts == v, ext_ref[start : start + rows + 2], moved)
        out_ref[c] = 0.5 * moved[1 : rows + 1] + 0.25 * (moved[:rows] + moved[2 : rows + 2])


def final_rows(mid, low, high, shifts):
    channels, rows, tile = mid.shape
    block = 256
    return pl.pallas_call(
        final_kernel,
        grid=(tile // block,),
        in_specs=[
            pl.BlockSpec((1, block), lambda i: (0, i)),
            pl.BlockSpec((channels, rows, block), lambda i: (0, 0, i)),
            pl.BlockSpec((channels, EDGE, block), lambda i: (0, 0, i)),
            pl.BlockSpec((channels, EDGE, block), lambda i: (0, 0, i)),
        ],
        out_specs=pl.BlockSpec((channels, rows, block), lambda i: (0, 0, i)),
        out_shape=jax.ShapeDtypeStruct((channels, rows, tile), F32),
        scratch_shapes=[pltpu.VMEM((rows + 2 * EDGE, block), F32)],
        name="final_rows",
    )(shifts, mid, low, high)


def neighbours(axis):
    count = lax.axis_size(axis)
    forward = [(i, i + 1) for i in range(count - 1)]
    return forward, [(b, a) for a, b in forward]


def swapped(value, axis, mask):
    pairs = [(source, source ^ mask) for source in range(lax.axis_size(axis))]
    return lax.ppermute(value, axis, pairs)


def classes_of(slab):
    top = -(-slab * RIM // GROUP) * GROUP
    rough = {int(slab * f) // GROUP * GROUP for f in (3.5, 4, 4.5, 5.5)}
    return sorted({h for h in rough if h >= 2 * GROUP} | {top})


def per_device(volume, shear_rows, shear_cols, warp_cols, warp_rows):
    channels, slab, rows, cols = volume.shape
    depth = lax.axis_size("depth")
    n_rows = lax.axis_size("rows")
    forward, backward = neighbours("rows")

    n_up = jnp.maximum(0, shear_rows + 1)
    n_dn = jnp.maximum(0, 1 - shear_rows)
    end_up = jnp.cumsum(n_up)
    end_dn = jnp.cumsum(n_dn)
    off_up = end_up - n_up
    off_dn = end_dn - n_dn
    need = jnp.maximum(end_up[-1], end_dn[-1]).astype(jnp.int32)
    for other in [swapped(need, "depth", m) for m in range(1, depth)]:
        need = jnp.maximum(need, other)
    row = jnp.arange(EDGE, dtype=jnp.int32)
    at_up = jnp.where(row[None] < n_up[:, None], off_up[:, None] + row[None], -1).reshape(1, -1)
    back = row[None] - (EDGE - n_dn[:, None])
    at_dn = jnp.where(back >= 0, off_dn[:, None] + back, -1).reshape(1, -1)
    row_start = lax.axis_index("rows") * rows
    warp = lax.dynamic_slice_in_dim(warp_cols, row_start, rows, 0).reshape(rows, 1)
    scalars = (shear_rows, shear_cols, off_up, off_dn)

    sizes = classes_of(slab)
    which = sum((need > size).astype(jnp.int32) for size in sizes[:-1])
    branches = [
        functools.partial(slab_stage, size, number + 1, depth, n_rows)
        for number, size in enumerate(sizes)
    ]
    mid, low, high = lax.switch(which, branches, volume, scalars, at_up, at_dn, warp)
    under = lax.ppermute(high, "rows", forward)
    above = lax.ppermute(low, "rows", backward)
    return final_rows(mid, under, above, warp_rows.reshape(1, -1))


def solution(mesh):
    return jax.shard_map(
        per_device,
        mesh=mesh,
        in_specs=(P(None, "depth", "rows", None), P("depth"), P("depth"), P(), P("depth")),
        out_specs=P(None, "rows", "depth"),
        check_vma=False,
    )
```

```python
import functools

import jax
import jax.numpy as jnp
from jax import lax
from jax.experimental import pallas as pl
from jax.experimental.pallas import tpu as pltpu
from jax.sharding import PartitionSpec as P

SHIFT = 8
RIM = SHIFT + 1
GROUP = 16
EDGE = 16
LANES = 128
LEAD = 16
CHUNK = 512
BLOCK = 8
SLOT = 10
AHEAD = 4
GHOST_LAG = 2
MERGE_LAG = 4
BF = jnp.bfloat16
F32 = jnp.float32
MESH = pl.DeviceIdType.MESH


def weight_of(offset):
    return jnp.where(offset == 0, 0.5, jnp.where(jnp.abs(offset) == 1, 0.25, 0.0)).astype(F32)


def iota(shape, dim):
    return lax.broadcasted_iota(jnp.int32, shape, dim)


def slab_kernel(
    sizes, row_s, col_s, off_up, off_dn, at_ref, slot_ref, warp_ref, vol_hbm,
    mid_ref, low_ref, high_ref,
    vol, a_send, a_recv, t_send, t_recv, c_send, c_recv, spread, own_w, colour_w, w_col, unpack, collect,
    pick_a, pick_t, band_a, band_c, trans, t_all, ghost, acc, outb, parts, wide_ref,
    load_sem, a_ss, a_rs, t_ss, t_rs, c_ss, c_rs, s_part, r_part,
):
    depth, n_rows = sizes
    chunks, channels, slab, rows, _ = vol.shape
    colours = channels - 1
    high = a_send.shape[2]
    cols = chunks * CHUNK
    tile = cols // depth
    per = CHUNK // LANES
    per_tile = tile // LANES
    pieces = tile // CHUNK
    flat = channels * rows
    tint = colours * rows
    step = BLOCK * rows
    me = lax.axis_index("depth")
    row = lax.axis_index("rows")
    has = (row > 0, row < n_rows - 1)
    got = (row < n_rows - 1, row > 0)
    target = (jnp.maximum(row - 1, 0), jnp.minimum(row + 1, n_rows - 1))

    def load_alpha(i):
        at = pl.ds(pl.multiple_of(i * CHUNK, CHUNK), CHUNK)
        return pltpu.make_async_copy(vol_hbm.at[colours, :, :, at], vol.at[i, colours], load_sem.at[0, i])

    def load_colour(i):
        at = pl.ds(pl.multiple_of(i * CHUNK, CHUNK), CHUNK)
        return pltpu.make_async_copy(
            vol_hbm.at[pl.ds(0, colours), :, :, at], vol.at[i, pl.ds(0, colours)], load_sem.at[1, i]
        )

    order = [chunks - 1] + list(range(chunks - 1))
    for i in order:
        load_alpha(i).start()
    for i in order:
        load_colour(i).start()

    barrier = pltpu.get_barrier_semaphore()
    for r in (lax.rem(row + 1, n_rows), lax.rem(row + n_rows - 1, n_rows)):
        pl.semaphore_signal(barrier, inc=1, device_id=(me, r), device_id_type=MESH)
    for m in range(1, depth):
        pl.semaphore_signal(barrier, inc=1, device_id=(lax.rem(me + m, depth), row), device_id_type=MESH)
    pl.semaphore_wait(barrier, depth + 1)

    def message(kind, way, i):
        source, dest, ss, rs = kind
        return pltpu.make_async_remote_copy(
            source.at[way, i], dest.at[way, i], ss.at[way, i], rs.at[way, i],
            device_id=(me, target[way]), device_id_type=MESH,
        )

    def lead_message(way):
        part = pl.ds(0, LANES)
        return pltpu.make_async_remote_copy(
            a_send.at[way, chunks, :, part], a_recv.at[way, chunks, :, part],
            a_ss.at[way, chunks], a_rs.at[way, chunks],
            device_id=(me, target[way]), device_id_type=MESH,
        )

    kind_a = (a_send, a_recv, a_ss, a_rs)
    kind_t = (t_send, t_recv, t_ss, t_rs)
    kind_c = (c_send, c_recv, c_ss, c_rs)

    def start(kind, i):
        for way in range(2):
            @pl.when(has[way])
            def _():
                message(kind, way, i).start()

    def arrived(kind, i):
        for way in range(2):
            @pl.when(got[way])
            def _():
                message(kind, way, i).wait_recv()

    def sent(kind, i):
        for way in range(2):
            @pl.when(has[way])
            def _():
                message(kind, way, i).wait_send()

    firsts = (0, rows - EDGE)
    for way in range(2):
        slots = at_ref[way : way + 1]
        pick_a[way] = (iota((high, slab * EDGE), 0) == slots).astype(F32).astype(BF)

    def pack(i, way, at):
        first = firsts[way]
        source = vol[i, colours, :, first : first + EDGE, at : CHUNK]
        source = source.reshape(slab * EDGE, CHUNK - at)
        return jnp.dot(pick_a[way], source, preferred_element_type=F32).astype(BF)

    load_alpha(chunks - 1).wait()
    for way in range(2):
        a_send[way, chunks, :, :LANES] = pack(chunks - 1, way, CHUNK - LANES)

    @pl.loop(0, chunks)
    def _(i):
        @pl.when(i < chunks - 1)
        def _():
            load_alpha(i).wait()

        for way in range(2):
            a_send[way, i] = pack(i, way, 0)

        @pl.when(i == 0)
        def _():
            for way in range(2):
                @pl.when(has[way])
                def _():
                    lead_message(way).start()

        @pl.when((i > 0) & (i <= AHEAD))
        def _():
            start(kind_a, i - 1)

    for way in range(2):
        @pl.when(jnp.logical_not(got[way]))
        def _():
            a_recv[way] = jnp.zeros(a_recv.shape[1:], BF)
            t_recv[way] = jnp.zeros(t_recv.shape[1:], BF)
            c_recv[way] = jnp.zeros(c_recv.shape[1:], BF)

    lane = iota((high, slab * rows), 0)
    for way in range(2):
        slots = slot_ref[way : way + 1]
        pick_t[way * high : (way + 1) * high] = (lane == slots).astype(F32).astype(BF)
    shape = (2 * rows, slab * rows)
    m = iota(shape, 0)
    j = iota(shape, 1)
    s = slot_ref[2:3]
    e = (j % rows) % SLOT
    side = jnp.where(s > 0, 0, jnp.where(s < 0, 1, jnp.where(e >= SHIFT // 2 + 1, 0, 1)))
    collect[...] = (((m % rows) + rows * (m // rows)) == ((j % rows) + rows * side)).astype(F32).astype(BF)

    @pl.loop(0, slab)
    def _(k):
        s = row_s[k]
        ou = off_up[k]
        od = off_dn[k]
        n_up = jnp.maximum(0, s + 1)
        n_dn = jnp.maximum(0, 1 - s)
        mine = pl.ds(pl.multiple_of(k * rows, rows), rows)
        y = iota((rows, high), 0)
        slot = iota((rows, high), 1)
        u = slot - ou
        keep = (u >= 0) & (u < n_up)
        spread[mine, :high] = jnp.where(keep, weight_of(rows + u - y - s), 0.0).astype(BF)
        v = slot - od
        keep = (v >= 0) & (v < n_dn)
        spread[mine, high:] = jnp.where(keep, weight_of(v - n_dn - y - s), 0.0).astype(BF)
        e = jnp.where(y < colours * SLOT, y % SLOT, -1 - 2 * rows)
        e = jnp.where(e > SHIFT, -1 - 2 * rows, e)
        hit = (v == e) & (v < n_dn) & (v >= 0)
        unpack[mine, :high] = hit.astype(F32).astype(BF)
        hit = (u == e - SHIFT + s) & (u < n_up) & (u >= 0)
        unpack[mine, high:] = hit.astype(F32).astype(BF)
        y = iota((rows, step), 0)
        j = iota((rows, step), 1)
        own_w[mine] = jnp.where(
            (j // rows) == lax.rem(k, BLOCK), weight_of((j % rows) - y - s), 0.0
        ).astype(BF)
        m = iota((flat, tint), 0)
        j = iota((flat, tint), 1)
        e = (m - tint) % SLOT
        north = jnp.where(s > 0, 1, jnp.where(s < 0, 0, jnp.where(e >= SHIFT // 2 + 1, 1, 0)))
        y = jnp.where(m < tint, m % rows, jnp.where(north > 0, e - RIM, rows + e))
        c = jnp.where(m < tint, m // rows, (m - tint) // SLOT)
        same = c == (j // rows)
        colour_w[k] = jnp.where(same, weight_of((j % rows) - y - s), 0.0).astype(BF)
        shape = (2 * LANES, LANES)
        m = iota(shape, 0)
        n = iota(shape, 1)
        w = weight_of(m - n - (LANES - LEAD) - col_s[k])
        w_col[0, k] = w.astype(BF)
        w_col[1, k] = jnp.where(jnp.where(m < LANES, 0, 1) == jnp.where(n < LEAD, 0, 1), w, 0.0).astype(BF)

    def alpha_rows(i, at, to, width):
        halo = jnp.concatenate([a_recv[way, i, :, :width] for way in range(2)], 0)
        source = i if at == 0 else chunks - 1
        for b in range(slab // BLOCK):
            part = slice(b * step, (b + 1) * step)
            own = vol[source, colours, b * BLOCK : (b + 1) * BLOCK, :, at : at + width]
            own = own.reshape(step, width)
            total = jnp.dot(own_w[part], own, preferred_element_type=F32)
            total = total + jnp.dot(spread[part], halo, preferred_element_type=F32)
            band_a[part, to : to + width] = total.astype(BF)

    def colour_rows(i, k, at, width):
        opacity = vol[i, colours, k, :, at : at + width]
        own = [vol[i, c, k, :, at : at + width] * opacity for c in range(colours)]
        return jnp.dot(colour_w[k], jnp.concatenate(own, 0), preferred_element_type=F32).astype(BF)

    for way in range(2):
        @pl.when(got[way])
        def _():
            lead_message(way).wait_recv()

    alpha_rows(chunks, CHUNK - LANES, CHUNK, LANES)
    load_colour(chunks - 1).wait()

    @pl.loop(0, slab)
    def _(k):
        band_c[k, :, CHUNK:] = colour_rows(chunks - 1, k, CHUNK - LANES, LANES)

    def composite(i):
        arrived(kind_a, i)

        @pl.when(i < chunks - 1)
        def _():
            load_colour(i).wait()

        band_a[:, :LANES] = band_a[:, CHUNK:]
        alpha_rows(i, 0, LANES, CHUNK)
        trans[...] = jnp.ones_like(trans)
        acc[i] = jnp.zeros(acc.shape[1:], F32)
        lead = jnp.where(i == 0, 1, 0)

        @pl.loop(0, slab, unroll=4)
        def _(k):
            mine = pl.ds(pl.multiple_of(k * rows, rows), rows)
            band_c[k, :, :LANES] = band_c[k, :, CHUNK:]
            band_c[k, :, LANES:] = colour_rows(i, k, 0, CHUNK)

            def window(w):
                at = slice(w * LANES, (w + 2) * LANES)
                return [band_a[mine, at], band_c[k, :, at]]

            first = jnp.dot(
                jnp.concatenate(window(0), 0), w_col[lead, k], preferred_element_type=F32
            )
            others = sum([window(w) for w in range(1, per)], [])
            rest = jnp.dot(jnp.concatenate(others, 0), w_col[0, k], preferred_element_type=F32)
            tall = rows + flat
            for w in range(per):
                sheared = first if w == 0 else rest[(w - 1) * tall : w * tall]
                at = slice(w * LANES, (w + 1) * LANES)
                t = trans[:, at]
                for c in range(colours):
                    acc[i, c * rows : (c + 1) * rows, at] += t * sheared[(c + 1) * rows : (c + 2) * rows]
                ghost[i, mine, at] = sheared[flat:].astype(BF)
                t_all[mine, at] = t.astype(BF)
                trans[:, at] = t - t * sheared[:rows]

        acc[i, tint:] = 1.0 - trans[...]
        picked = jnp.dot(pick_t[...], t_all[...], preferred_element_type=F32).astype(BF)
        t_send[0, i] = picked[:high]
        t_send[1, i] = picked[high:]

    def ghosts(i):
        arrived(kind_t, i)
        seen = jnp.concatenate([t_recv[0, i], t_recv[1, i]], 0)
        total = None
        for b in range(slab // BLOCK):
            part = slice(b * step, (b + 1) * step)
            t = jnp.dot(unpack[part], seen, preferred_element_type=F32)
            seen_colour = (t * ghost[i, part].astype(F32)).astype(BF)
            value = jnp.dot(collect[:, part], seen_colour, preferred_element_type=F32)
            total = value if total is None else total + value
        total = total.astype(BF)
        c_send[0, i] = total[:rows]
        c_send[1, i] = total[rows:]

    def merge(i):
        arrived(kind_c, i)
        m = iota((tint, 2 * rows), 0)
        j = iota((tint, 2 * rows), 1)
        e = (j % rows) % SLOT
        y = jnp.where(j < rows, rows - RIM + e, e)
        there = (m // rows == (j % rows) // SLOT) & (m % rows == y) & (e <= SHIFT)
        place = there.astype(F32).astype(BF)
        both = jnp.concatenate([c_recv[0, i], c_recv[1, i]], 0)
        more = jnp.dot(place, both, preferred_element_type=F32)
        image = jnp.concatenate([acc[i, :tint] + more, acc[i, tint:]], 0)
        for w in range(per):
            outb[i * per + w] = image[:, w * LANES : (w + 1) * LANES].astype(BF)

        @pl.when(i == 0)
        def _():
            piece = image[:, :LANES]
            n = iota((flat, LANES), 1)
            outb[chunks * per] = jnp.where(n < LEAD, piece, 0.0).astype(BF)
            outb[0] = jnp.where(n < LEAD, 0.0, piece).astype(BF)

    def part_copy(i, source, count, owner, at, margin):
        return pltpu.make_async_remote_copy(
            outb.at[pl.ds(source, count)],
            parts.at[me, pl.ds(at, count)],
            s_part.at[margin, i],
            r_part.at[me, pieces if margin else lax.rem(i, pieces)],
            device_id=(owner, row),
            device_id_type=MESH,
        )

    def deliver(i, act, keep):
        owner = i // pieces
        at = lax.rem(i, pieces) * per

        @pl.when(owner != me)
        def _():
            act(part_copy(i, i * per, per, owner, at, 0))

        if keep:
            @pl.when(owner == me)
            def _():
                parts[me, pl.ds(at, per)] = outb[pl.ds(i * per, per)]

        margin = lax.rem(i, pieces) == 0
        left = lax.rem(owner + depth - 1, depth)
        source = jnp.where(i == 0, chunks * per, i * per)

        @pl.when(margin & (left != me))
        def _():
            act(part_copy(i, source, 1, left, per_tile, 1))

        if keep:
            @pl.when(margin & (left == me))
            def _():
                parts[me, per_tile] = outb[source]

    @pl.loop(0, chunks + MERGE_LAG)
    def _(i):
        @pl.when(i < chunks)
        def _():
            composite(i)

        @pl.when((i >= GHOST_LAG) & (i < chunks + GHOST_LAG))
        def _():
            ghosts(i - GHOST_LAG)

        @pl.when(i < chunks)
        def _():
            start(kind_t, i)

        @pl.when(i + AHEAD < chunks)
        def _():
            start(kind_a, i + AHEAD)

        @pl.when(i > MERGE_LAG)
        def _():
            deliver(i - MERGE_LAG - 1, lambda copy: copy.start(), True)

        @pl.when(i >= MERGE_LAG)
        def _():
            merge(i - MERGE_LAG)

        @pl.when((i >= GHOST_LAG) & (i < chunks + GHOST_LAG))
        def _():
            start(kind_c, i - GHOST_LAG)

    deliver(jnp.int32(chunks - 1), lambda copy: copy.start(), True)

    for d in range(depth):
        @pl.when(me != d)
        def _():
            for p in range(pieces + 1):
                count = per if p < pieces else 1
                pltpu.make_async_remote_copy(
                    outb.at[pl.ds(0, count)],
                    parts.at[d, pl.ds(p * per, count)],
                    s_part.at[0, 0],
                    r_part.at[d, p],
                    device_id=(me, row),
                    device_id_type=MESH,
                ).wait_recv()

    for w in range(per_tile + 1):
        image = parts[0, w].astype(F32)
        image = image.reshape(channels, rows, LANES)
        for d in range(1, depth):
            back = parts[d, w].astype(F32).reshape(channels, rows, LANES)
            image = image + (1.0 - image[channels - 1 :]) * back
        wide_ref[:, w * LANES : (w + 1) * LANES] = image.reshape(flat, LANES)

    width = wide_ref.shape[1]
    amount = warp_ref[...] + SHIFT
    for c in range(channels):
        line = wide_ref[c * rows : (c + 1) * rows]
        line = 0.5 * line + 0.25 * (pltpu.roll(line, 1, 1) + pltpu.roll(line, width - 1, 1))
        line = pltpu.roll(line, width - (LEAD - SHIFT), 1)
        for bit in (1, 2, 4, 8, 16):
            line = jnp.where((amount & bit) != 0, pltpu.roll(line, width - bit, 1), line)
        across = line[:, :tile]
        mid_ref[c] = across
        low_ref[c] = across[:EDGE].astype(BF)
        high_ref[c] = across[rows - EDGE :].astype(BF)

    for way in range(2):
        @pl.when(has[way])
        def _():
            lead_message(way).wait_send()

    @pl.loop(0, chunks)
    def _(i):
        for kind in (kind_a, kind_t, kind_c):
            sent(kind, i)
        deliver(i, lambda copy: copy.wait_send(), False)


def slab_stage(high, number, depth, n_rows, volume, scalars, at, slots, warp):
    channels, slab, rows, cols = volume.shape
    chunks = cols // CHUNK
    per = CHUNK // LANES
    tile = cols // depth
    flat = channels * rows
    tint = flat - rows
    pieces = tile // CHUNK
    smem = pl.BlockSpec(memory_space=pltpu.SMEM)
    vmem = pl.BlockSpec(memory_space=pltpu.VMEM)
    half = jax.ShapeDtypeStruct((channels, EDGE, tile), BF)
    dma = pltpu.SemaphoreType.DMA
    return pl.pallas_call(
        functools.partial(slab_kernel, (depth, n_rows)),
        in_specs=[smem] * 4 + [vmem] * 3 + [pl.BlockSpec(memory_space=pl.ANY)],
        out_specs=[vmem] * 3,
        out_shape=[jax.ShapeDtypeStruct((channels, rows, tile), F32), half, half],
        scratch_shapes=[
            pltpu.VMEM((chunks, channels, slab, rows, CHUNK), BF),
            pltpu.VMEM((2, chunks + 1, high, CHUNK), BF),
            pltpu.VMEM((2, chunks + 1, high, CHUNK), BF),
            pltpu.VMEM((2, chunks, high, CHUNK), BF),
            pltpu.VMEM((2, chunks, high, CHUNK), BF),
            pltpu.VMEM((2, chunks, rows, CHUNK), BF),
            pltpu.VMEM((2, chunks, rows, CHUNK), BF),
            pltpu.VMEM((slab * rows, 2 * high), BF),
            pltpu.VMEM((slab * rows, BLOCK * rows), BF),
            pltpu.VMEM((slab, flat, tint), BF),
            pltpu.VMEM((2, slab, 2 * LANES, LANES), BF),
            pltpu.VMEM((slab * rows, 2 * high), BF),
            pltpu.VMEM((2 * rows, slab * rows), BF),
            pltpu.VMEM((2, high, slab * EDGE), BF),
            pltpu.VMEM((2 * high, slab * rows), BF),
            pltpu.VMEM((slab * rows, LANES + CHUNK), BF),
            pltpu.VMEM((slab, flat, LANES + CHUNK), BF),
            pltpu.VMEM((rows, CHUNK), F32),
            pltpu.VMEM((slab * rows, CHUNK), BF),
            pltpu.VMEM((chunks, slab * rows, CHUNK), BF),
            pltpu.VMEM((chunks, flat, CHUNK), F32),
            pltpu.VMEM((chunks * per + 1, flat, LANES), BF),
            pltpu.VMEM((depth, tile // LANES + 1, flat, LANES), BF),
            pltpu.VMEM((flat, tile + LANES), F32),
            dma((2, chunks)),
            dma((2, chunks + 1)),
            dma((2, chunks + 1)),
            dma((2, chunks)),
            dma((2, chunks)),
            dma((2, chunks)),
            dma((2, chunks)),
            dma((2, chunks)),
            dma((depth, pieces + 1)),
        ],
        compiler_params=pltpu.CompilerParams(
            collective_id=number, has_side_effects=True, vmem_limit_bytes=60 * 2**20
        ),
        name=f"slab_{high}",
    )(*scalars, at, slots, warp, volume)


def final_kernel(shift_ref, mid_ref, low_ref, high_ref, out_ref, ext_ref):
    channels, rows, tile = mid_ref.shape
    shifts = shift_ref[...]
    for c in range(channels):
        ext_ref[:EDGE] = low_ref[c].astype(F32)
        ext_ref[EDGE : EDGE + rows] = mid_ref[c]
        ext_ref[EDGE + rows :] = high_ref[c].astype(F32)
        moved = jnp.zeros((rows + 2, tile), F32)
        for v in range(-SHIFT, SHIFT + 1):
            start = EDGE + v - 1
            moved = jnp.where(shifts == v, ext_ref[start : start + rows + 2], moved)
        out_ref[c] = 0.5 * moved[1 : rows + 1] + 0.25 * (moved[:rows] + moved[2 : rows + 2])


def final_rows(mid, low, high, shifts):
    channels, rows, tile = mid.shape
    block = 256
    return pl.pallas_call(
        final_kernel,
        grid=(tile // block,),
        in_specs=[
            pl.BlockSpec((1, block), lambda i: (0, i)),
            pl.BlockSpec((channels, rows, block), lambda i: (0, 0, i)),
            pl.BlockSpec((channels, EDGE, block), lambda i: (0, 0, i)),
            pl.BlockSpec((channels, EDGE, block), lambda i: (0, 0, i)),
        ],
        out_specs=pl.BlockSpec((channels, rows, block), lambda i: (0, 0, i)),
        out_shape=jax.ShapeDtypeStruct((channels, rows, tile), F32),
        scratch_shapes=[pltpu.VMEM((rows + 2 * EDGE, block), F32)],
        name="final_rows",
    )(shifts, mid, low, high)


def neighbours(axis):
    count = lax.axis_size(axis)
    forward = [(i, i + 1) for i in range(count - 1)]
    return forward, [(b, a) for a, b in forward]


def swapped(value, axis, mask):
    pairs = [(source, source ^ mask) for source in range(lax.axis_size(axis))]
    return lax.ppermute(value, axis, pairs)


def classes_of(slab):
    top = -(-slab * RIM // GROUP) * GROUP
    rough = {int(slab * f) // GROUP * GROUP for f in (3, 4, 5, 6)}
    return sorted({h for h in rough if h >= 2 * GROUP} | {top})


def per_device(volume, shear_rows, shear_cols, warp_cols, warp_rows):
    channels, slab, rows, cols = volume.shape
    depth = lax.axis_size("depth")
    n_rows = lax.axis_size("rows")
    forward, backward = neighbours("rows")

    n_up = jnp.maximum(0, shear_rows + 1)
    n_dn = jnp.maximum(0, 1 - shear_rows)
    end_up = jnp.cumsum(n_up)
    end_dn = jnp.cumsum(n_dn)
    off_up = end_up - n_up
    off_dn = end_dn - n_dn
    need = jnp.maximum(end_up[-1], end_dn[-1]).astype(jnp.int32)
    for other in [swapped(need, "depth", m) for m in range(1, depth)]:
        need = jnp.maximum(need, other)
    row = jnp.arange(EDGE, dtype=jnp.int32)
    at_up = jnp.where(row[None] < n_up[:, None], off_up[:, None] + row[None], -1)
    back = row[None] - (EDGE - n_dn[:, None])
    at_dn = jnp.where(back >= 0, off_dn[:, None] + back, -1)
    at = jnp.stack([at_up, at_dn]).reshape(2, -1)
    y = jnp.arange(rows, dtype=jnp.int32)[None]
    north = jnp.where(y < n_dn[:, None], off_dn[:, None] + y, -1)
    back = y - (rows - n_up[:, None])
    south = jnp.where(back >= 0, off_up[:, None] + back, -1)
    slots = jnp.stack([north, south, jnp.broadcast_to(shear_rows[:, None], north.shape)]).reshape(3, -1)
    row_start = lax.axis_index("rows") * rows
    warp = lax.dynamic_slice_in_dim(warp_cols, row_start, rows, 0).reshape(rows, 1)
    scalars = (shear_rows, shear_cols, off_up, off_dn)

    sizes = classes_of(slab)
    which = sum((need > size).astype(jnp.int32) for size in sizes[:-1])
    branches = [
        functools.partial(slab_stage, size, number + 1, depth, n_rows)
        for number, size in enumerate(sizes)
    ]
    mid, low, high = lax.switch(which, branches, volume, scalars, at, slots, warp)
    under = lax.ppermute(high, "rows", forward)
    above = lax.ppermute(low, "rows", backward)
    return final_rows(mid, under, above, warp_rows.reshape(1, -1))


def solution(mesh):
    return jax.shard_map(
        per_device,
        mesh=mesh,
        in_specs=(P(None, "depth", "rows", None), P("depth"), P("depth"), P(), P("depth")),
        out_specs=P(None, "rows", "depth"),
        check_vma=False,
    )
```

```python
import functools

import jax
import jax.numpy as jnp
from jax import lax
from jax.experimental import pallas as pl
from jax.experimental.pallas import tpu as pltpu
from jax.sharding import PartitionSpec as P

SHIFT = 8
RIM = SHIFT + 1
GROUP = 16
EDGE = 16
LANES = 128
LEAD = 16
CHUNK = 512
BLOCK = 8
SLOT = 10
AHEAD = 4
GHOST_LAG = 2
MERGE_LAG = 4
BF = jnp.bfloat16
F32 = jnp.float32
MESH = pl.DeviceIdType.MESH


def weight_of(offset):
    return jnp.where(offset == 0, 0.5, jnp.where(jnp.abs(offset) == 1, 0.25, 0.0)).astype(F32)


def iota(shape, dim):
    return lax.broadcasted_iota(jnp.int32, shape, dim)


def slab_kernel(
    sizes, row_s, col_s, off_up, off_dn, at_ref, slot_ref, warp_ref, turn_ref, vol_hbm,
    out_ref,
    vol, a_send, a_recv, t_send, t_recv, c_send, c_recv, spread, own_w, colour_w, w_col, unpack, collect,
    pick_a, pick_t, band_a, band_c, trans, t_all, ghost, acc, outb, parts, wide_ref, f_send, f_recv,
    load_sem, a_ss, a_rs, t_ss, t_rs, c_ss, c_rs, s_part, r_part, f_ss, f_rs,
):
    depth, n_rows = sizes
    chunks, channels, slab, rows, _ = vol.shape
    colours = channels - 1
    high = a_send.shape[2]
    cols = chunks * CHUNK
    tile = cols // depth
    per = CHUNK // LANES
    per_tile = tile // LANES
    pieces = tile // CHUNK
    flat = channels * rows
    tint = colours * rows
    step = BLOCK * rows
    me = lax.axis_index("depth")
    row = lax.axis_index("rows")
    has = (row > 0, row < n_rows - 1)
    got = (row < n_rows - 1, row > 0)
    target = (jnp.maximum(row - 1, 0), jnp.minimum(row + 1, n_rows - 1))

    def load_alpha(i):
        at = pl.ds(pl.multiple_of(i * CHUNK, CHUNK), CHUNK)
        return pltpu.make_async_copy(vol_hbm.at[colours, :, :, at], vol.at[i, colours], load_sem.at[0, i])

    def load_colour(i):
        at = pl.ds(pl.multiple_of(i * CHUNK, CHUNK), CHUNK)
        return pltpu.make_async_copy(
            vol_hbm.at[pl.ds(0, colours), :, :, at], vol.at[i, pl.ds(0, colours)], load_sem.at[1, i]
        )

    order = [chunks - 1] + list(range(chunks - 1))
    for i in order:
        load_alpha(i).start()
    for i in order:
        load_colour(i).start()

    barrier = pltpu.get_barrier_semaphore()
    for r in (lax.rem(row + 1, n_rows), lax.rem(row + n_rows - 1, n_rows)):
        pl.semaphore_signal(barrier, inc=1, device_id=(me, r), device_id_type=MESH)
    for m in range(1, depth):
        pl.semaphore_signal(barrier, inc=1, device_id=(lax.rem(me + m, depth), row), device_id_type=MESH)
    pl.semaphore_wait(barrier, depth + 1)

    def message(kind, way, i):
        source, dest, ss, rs = kind
        return pltpu.make_async_remote_copy(
            source.at[way, i], dest.at[way, i], ss.at[way, i], rs.at[way, i],
            device_id=(me, target[way]), device_id_type=MESH,
        )

    def lead_message(way):
        part = pl.ds(0, LANES)
        return pltpu.make_async_remote_copy(
            a_send.at[way, chunks, :, part], a_recv.at[way, chunks, :, part],
            a_ss.at[way, chunks], a_rs.at[way, chunks],
            device_id=(me, target[way]), device_id_type=MESH,
        )

    kind_a = (a_send, a_recv, a_ss, a_rs)
    kind_t = (t_send, t_recv, t_ss, t_rs)
    kind_c = (c_send, c_recv, c_ss, c_rs)
    kind_f = (f_send, f_recv, f_ss, f_rs)

    def start(kind, i):
        for way in range(2):
            @pl.when(has[way])
            def _():
                message(kind, way, i).start()

    def arrived(kind, i):
        for way in range(2):
            @pl.when(got[way])
            def _():
                message(kind, way, i).wait_recv()

    def sent(kind, i):
        for way in range(2):
            @pl.when(has[way])
            def _():
                message(kind, way, i).wait_send()

    firsts = (0, rows - EDGE)
    for way in range(2):
        slots = at_ref[way : way + 1]
        pick_a[way] = (iota((high, slab * EDGE), 0) == slots).astype(F32).astype(BF)

    def pack(i, way, at):
        first = firsts[way]
        source = vol[i, colours, :, first : first + EDGE, at : CHUNK]
        source = source.reshape(slab * EDGE, CHUNK - at)
        return jnp.dot(pick_a[way], source, preferred_element_type=F32).astype(BF)

    load_alpha(chunks - 1).wait()
    for way in range(2):
        a_send[way, chunks, :, :LANES] = pack(chunks - 1, way, CHUNK - LANES)

    @pl.loop(0, chunks)
    def _(i):
        @pl.when(i < chunks - 1)
        def _():
            load_alpha(i).wait()

        for way in range(2):
            a_send[way, i] = pack(i, way, 0)

        @pl.when(i == 0)
        def _():
            for way in range(2):
                @pl.when(has[way])
                def _():
                    lead_message(way).start()

        @pl.when((i > 0) & (i <= AHEAD))
        def _():
            start(kind_a, i - 1)

    for way in range(2):
        @pl.when(jnp.logical_not(got[way]))
        def _():
            a_recv[way] = jnp.zeros(a_recv.shape[1:], BF)
            t_recv[way] = jnp.zeros(t_recv.shape[1:], BF)
            c_recv[way] = jnp.zeros(c_recv.shape[1:], BF)
            f_recv[way] = jnp.zeros(f_recv.shape[1:], BF)

    lane = iota((high, slab * rows), 0)
    for way in range(2):
        slots = slot_ref[way : way + 1]
        pick_t[way * high : (way + 1) * high] = (lane == slots).astype(F32).astype(BF)
    shape = (2 * rows, slab * rows)
    m = iota(shape, 0)
    j = iota(shape, 1)
    s = slot_ref[2:3]
    e = (j % rows) % SLOT
    side = jnp.where(s > 0, 0, jnp.where(s < 0, 1, jnp.where(e >= SHIFT // 2 + 1, 0, 1)))
    collect[...] = (((m % rows) + rows * (m // rows)) == ((j % rows) + rows * side)).astype(F32).astype(BF)

    @pl.loop(0, slab)
    def _(k):
        s = row_s[k]
        ou = off_up[k]
        od = off_dn[k]
        n_up = jnp.maximum(0, s + 1)
        n_dn = jnp.maximum(0, 1 - s)
        mine = pl.ds(pl.multiple_of(k * rows, rows), rows)
        y = iota((rows, high), 0)
        slot = iota((rows, high), 1)
        u = slot - ou
        keep = (u >= 0) & (u < n_up)
        spread[mine, :high] = jnp.where(keep, weight_of(rows + u - y - s), 0.0).astype(BF)
        v = slot - od
        keep = (v >= 0) & (v < n_dn)
        spread[mine, high:] = jnp.where(keep, weight_of(v - n_dn - y - s), 0.0).astype(BF)
        e = jnp.where(y < colours * SLOT, y % SLOT, -1 - 2 * rows)
        e = jnp.where(e > SHIFT, -1 - 2 * rows, e)
        hit = (v == e) & (v < n_dn) & (v >= 0)
        unpack[mine, :high] = hit.astype(F32).astype(BF)
        hit = (u == e - SHIFT + s) & (u < n_up) & (u >= 0)
        unpack[mine, high:] = hit.astype(F32).astype(BF)
        y = iota((rows, step), 0)
        j = iota((rows, step), 1)
        own_w[mine] = jnp.where(
            (j // rows) == lax.rem(k, BLOCK), weight_of((j % rows) - y - s), 0.0
        ).astype(BF)
        m = iota((flat, tint), 0)
        j = iota((flat, tint), 1)
        e = (m - tint) % SLOT
        north = jnp.where(s > 0, 1, jnp.where(s < 0, 0, jnp.where(e >= SHIFT // 2 + 1, 1, 0)))
        y = jnp.where(m < tint, m % rows, jnp.where(north > 0, e - RIM, rows + e))
        c = jnp.where(m < tint, m // rows, (m - tint) // SLOT)
        same = c == (j // rows)
        colour_w[k] = jnp.where(same, weight_of((j % rows) - y - s), 0.0).astype(BF)
        shape = (2 * LANES, LANES)
        m = iota(shape, 0)
        n = iota(shape, 1)
        w = weight_of(m - n - (LANES - LEAD) - col_s[k])
        w_col[0, k] = w.astype(BF)
        w_col[1, k] = jnp.where(jnp.where(m < LANES, 0, 1) == jnp.where(n < LEAD, 0, 1), w, 0.0).astype(BF)

    def alpha_rows(i, at, to, width):
        halo = jnp.concatenate([a_recv[way, i, :, :width] for way in range(2)], 0)
        source = i if at == 0 else chunks - 1
        for b in range(slab // BLOCK):
            part = slice(b * step, (b + 1) * step)
            own = vol[source, colours, b * BLOCK : (b + 1) * BLOCK, :, at : at + width]
            own = own.reshape(step, width)
            total = jnp.dot(own_w[part], own, preferred_element_type=F32)
            total = total + jnp.dot(spread[part], halo, preferred_element_type=F32)
            band_a[part, to : to + width] = total.astype(BF)

    def colour_rows(i, k, at, width):
        opacity = vol[i, colours, k, :, at : at + width]
        own = [vol[i, c, k, :, at : at + width] * opacity for c in range(colours)]
        return jnp.dot(colour_w[k], jnp.concatenate(own, 0), preferred_element_type=F32).astype(BF)

    for way in range(2):
        @pl.when(got[way])
        def _():
            lead_message(way).wait_recv()

    alpha_rows(chunks, CHUNK - LANES, CHUNK, LANES)
    load_colour(chunks - 1).wait()

    @pl.loop(0, slab)
    def _(k):
        band_c[k, :, CHUNK:] = colour_rows(chunks - 1, k, CHUNK - LANES, LANES)

    def composite(i):
        arrived(kind_a, i)

        @pl.when(i < chunks - 1)
        def _():
            load_colour(i).wait()

        band_a[:, :LANES] = band_a[:, CHUNK:]
        alpha_rows(i, 0, LANES, CHUNK)
        trans[...] = jnp.ones_like(trans)
        acc[i] = jnp.zeros(acc.shape[1:], F32)
        lead = jnp.where(i == 0, 1, 0)

        @pl.loop(0, slab, unroll=4)
        def _(k):
            band_c[k, :, :LANES] = band_c[k, :, CHUNK:]
            band_c[k, :, LANES:] = colour_rows(i, k, 0, CHUNK)

        @pl.loop(0, slab, unroll=4)
        def _(k):
            mine = pl.ds(pl.multiple_of(k * rows, rows), rows)

            def window(w):
                at = slice(w * LANES, (w + 2) * LANES)
                return [band_a[mine, at], band_c[k, :, at]]

            first = jnp.dot(
                jnp.concatenate(window(0), 0), w_col[lead, k], preferred_element_type=F32
            )
            others = sum([window(w) for w in range(1, per)], [])
            rest = jnp.dot(jnp.concatenate(others, 0), w_col[0, k], preferred_element_type=F32)
            tall = rows + flat
            for w in range(per):
                sheared = first if w == 0 else rest[(w - 1) * tall : w * tall]
                at = slice(w * LANES, (w + 1) * LANES)
                t = trans[:, at]
                for c in range(colours):
                    acc[i, c * rows : (c + 1) * rows, at] += t * sheared[(c + 1) * rows : (c + 2) * rows]
                ghost[i, mine, at] = sheared[flat:].astype(BF)
                t_all[mine, at] = t.astype(BF)
                trans[:, at] = t - t * sheared[:rows]

        acc[i, tint:] = 1.0 - trans[...]
        picked = jnp.dot(pick_t[...], t_all[...], preferred_element_type=F32).astype(BF)
        t_send[0, i] = picked[:high]
        t_send[1, i] = picked[high:]

    def ghosts(i):
        arrived(kind_t, i)
        seen = jnp.concatenate([t_recv[0, i], t_recv[1, i]], 0)
        total = None
        for b in range(slab // BLOCK):
            part = slice(b * step, (b + 1) * step)
            t = jnp.dot(unpack[part], seen, preferred_element_type=F32)
            seen_colour = (t * ghost[i, part].astype(F32)).astype(BF)
            value = jnp.dot(collect[:, part], seen_colour, preferred_element_type=F32)
            total = value if total is None else total + value
        total = total.astype(BF)
        c_send[0, i] = total[:rows]
        c_send[1, i] = total[rows:]

    def merge(i):
        arrived(kind_c, i)
        m = iota((tint, 2 * rows), 0)
        j = iota((tint, 2 * rows), 1)
        e = (j % rows) % SLOT
        y = jnp.where(j < rows, rows - RIM + e, e)
        there = (m // rows == (j % rows) // SLOT) & (m % rows == y) & (e <= SHIFT)
        place = there.astype(F32).astype(BF)
        both = jnp.concatenate([c_recv[0, i], c_recv[1, i]], 0)
        more = jnp.dot(place, both, preferred_element_type=F32)
        image = jnp.concatenate([acc[i, :tint] + more, acc[i, tint:]], 0)
        for w in range(per):
            outb[i * per + w] = image[:, w * LANES : (w + 1) * LANES].astype(BF)

        @pl.when(i == 0)
        def _():
            piece = image[:, :LANES]
            n = iota((flat, LANES), 1)
            outb[chunks * per] = jnp.where(n < LEAD, piece, 0.0).astype(BF)
            outb[0] = jnp.where(n < LEAD, 0.0, piece).astype(BF)

    def part_copy(i, source, count, owner, at, margin):
        return pltpu.make_async_remote_copy(
            outb.at[pl.ds(source, count)],
            parts.at[me, pl.ds(at, count)],
            s_part.at[margin, i],
            r_part.at[me, pieces if margin else lax.rem(i, pieces)],
            device_id=(owner, row),
            device_id_type=MESH,
        )

    def deliver(i, act, keep):
        owner = i // pieces
        at = lax.rem(i, pieces) * per

        @pl.when(owner != me)
        def _():
            act(part_copy(i, i * per, per, owner, at, 0))

        if keep:
            @pl.when(owner == me)
            def _():
                parts[me, pl.ds(at, per)] = outb[pl.ds(i * per, per)]

        margin = lax.rem(i, pieces) == 0
        left = lax.rem(owner + depth - 1, depth)
        source = jnp.where(i == 0, chunks * per, i * per)

        @pl.when(margin & (left != me))
        def _():
            act(part_copy(i, source, 1, left, per_tile, 1))

        if keep:
            @pl.when(margin & (left == me))
            def _():
                parts[me, per_tile] = outb[source]

    @pl.loop(0, chunks + MERGE_LAG)
    def _(i):
        @pl.when(i < chunks)
        def _():
            composite(i)

        @pl.when((i >= GHOST_LAG) & (i < chunks + GHOST_LAG))
        def _():
            ghosts(i - GHOST_LAG)

        @pl.when(i < chunks)
        def _():
            start(kind_t, i)

        @pl.when(i + AHEAD < chunks)
        def _():
            start(kind_a, i + AHEAD)

        @pl.when(i > MERGE_LAG)
        def _():
            deliver(i - MERGE_LAG - 1, lambda copy: copy.start(), True)

        @pl.when(i >= MERGE_LAG)
        def _():
            merge(i - MERGE_LAG)

        @pl.when((i >= GHOST_LAG) & (i < chunks + GHOST_LAG))
        def _():
            start(kind_c, i - GHOST_LAG)

    deliver(jnp.int32(chunks - 1), lambda copy: copy.start(), True)

    for d in range(depth):
        @pl.when(me != d)
        def _():
            for p in range(pieces + 1):
                count = per if p < pieces else 1
                pltpu.make_async_remote_copy(
                    outb.at[pl.ds(0, count)],
                    parts.at[d, pl.ds(p * per, count)],
                    s_part.at[0, 0],
                    r_part.at[d, p],
                    device_id=(me, row),
                    device_id_type=MESH,
                ).wait_recv()

    for w in range(per_tile + 1):
        image = parts[0, w].astype(F32)
        image = image.reshape(channels, rows, LANES)
        for d in range(1, depth):
            back = parts[d, w].astype(F32).reshape(channels, rows, LANES)
            image = image + (1.0 - image[channels - 1 :]) * back
        wide_ref[:, w * LANES : (w + 1) * LANES] = image.reshape(flat, LANES)

    amount = warp_ref[...] + SHIFT
    packed = f_send.shape[2]
    m = iota((packed, flat), 0)
    j = iota((packed, flat), 1)
    picks = []
    for first in (0, rows - RIM):
        there = (m // RIM == j // rows) & (m % RIM + first == j % rows)
        picks.append(there.astype(F32).astype(BF))
    width = CHUNK + LANES
    for h in range(pieces):
        lines = []
        for c in range(channels):
            line = wide_ref[c * rows : (c + 1) * rows, h * CHUNK : h * CHUNK + width]
            line = 0.5 * line + 0.25 * (pltpu.roll(line, 1, 1) + pltpu.roll(line, width - 1, 1))
            line = pltpu.roll(line, width - (LEAD - SHIFT), 1)
            for bit in (1, 2, 4, 8, 16):
                line = jnp.where((amount & bit) != 0, pltpu.roll(line, width - bit, 1), line)
            lines.append(line[:, :CHUNK])
        across = jnp.concatenate(lines, 0)
        wide_ref[:, h * CHUNK : (h + 1) * CHUNK] = across
        across = across.astype(BF)
        for way in range(2):
            f_send[way, h] = jnp.dot(picks[way], across, preferred_element_type=F32).astype(BF)
        if h > 0:
            start(kind_f, h - 1)
    start(kind_f, pieces - 1)

    half = rows // 2
    m = iota((flat, 2 * packed), 0)
    j = iota((flat, 2 * packed), 1)
    a = m % rows
    e = jnp.where(j < packed, a - half + RIM, a - half)
    slot = jnp.where(j < packed, j, j - packed)
    wanted = jnp.where(a < half, jnp.where(j < packed, e, -1), jnp.where(j < packed, -1, e))
    place = (slot // RIM == m // rows) & (slot % RIM == wanted)
    place = place.astype(F32).astype(BF)
    for h in range(pieces):
        arrived(kind_f, h)
        at = slice(h * CHUNK, (h + 1) * CHUNK)
        rim = jnp.concatenate([f_recv[1, h], f_recv[0, h]], 0)
        rim = jnp.dot(place, rim, preferred_element_type=F32)
        turn = turn_ref[:, at] + SHIFT
        for c in range(channels):
            low = rim[c * rows : c * rows + half]
            high_rows = rim[c * rows + half : (c + 1) * rows]
            ext = jnp.concatenate([low, wide_ref[c * rows : (c + 1) * rows, at], high_rows], 0)
            tall = ext.shape[0]
            ext = 0.5 * ext + 0.25 * (pltpu.roll(ext, 1, 0) + pltpu.roll(ext, tall - 1, 0))
            line = ext[half - SHIFT :]
            keep = rows + 2 * SHIFT
            line = jnp.where((turn & 8) != 0, line[8 : 8 + keep], line[:keep])
            far = jnp.concatenate([line[16 : 16 + rows], line[16 + rows - 8 : 16 + rows]], 0)
            line = jnp.where((turn & 16) != 0, far, line[: rows + 8])
            tall = rows + 8
            for bit in (4, 2, 1):
                line = jnp.where((turn & bit) != 0, pltpu.roll(line, tall - bit, 0), line)
            out_ref[c, :, at] = line[:rows]

    for way in range(2):
        @pl.when(has[way])
        def _():
            lead_message(way).wait_send()

    @pl.loop(0, chunks)
    def _(i):
        for kind in (kind_a, kind_t, kind_c):
            sent(kind, i)
        deliver(i, lambda copy: copy.wait_send(), False)

    for h in range(pieces):
        sent(kind_f, h)


def slab_stage(high, number, depth, n_rows, volume, scalars, at, slots, warp, turn):
    channels, slab, rows, cols = volume.shape
    chunks = cols // CHUNK
    per = CHUNK // LANES
    tile = cols // depth
    flat = channels * rows
    tint = flat - rows
    pieces = tile // CHUNK
    smem = pl.BlockSpec(memory_space=pltpu.SMEM)
    vmem = pl.BlockSpec(memory_space=pltpu.VMEM)
    packed = -(-channels * RIM // EDGE) * EDGE
    dma = pltpu.SemaphoreType.DMA
    return pl.pallas_call(
        functools.partial(slab_kernel, (depth, n_rows)),
        in_specs=[smem] * 4 + [vmem] * 4 + [pl.BlockSpec(memory_space=pl.ANY)],
        out_specs=vmem,
        out_shape=jax.ShapeDtypeStruct((channels, rows, tile), F32),
        scratch_shapes=[
            pltpu.VMEM((chunks, channels, slab, rows, CHUNK), BF),
            pltpu.VMEM((2, chunks + 1, high, CHUNK), BF),
            pltpu.VMEM((2, chunks + 1, high, CHUNK), BF),
            pltpu.VMEM((2, chunks, high, CHUNK), BF),
            pltpu.VMEM((2, chunks, high, CHUNK), BF),
            pltpu.VMEM((2, chunks, rows, CHUNK), BF),
            pltpu.VMEM((2, chunks, rows, CHUNK), BF),
            pltpu.VMEM((slab * rows, 2 * high), BF),
            pltpu.VMEM((slab * rows, BLOCK * rows), BF),
            pltpu.VMEM((slab, flat, tint), BF),
            pltpu.VMEM((2, slab, 2 * LANES, LANES), BF),
            pltpu.VMEM((slab * rows, 2 * high), BF),
            pltpu.VMEM((2 * rows, slab * rows), BF),
            pltpu.VMEM((2, high, slab * EDGE), BF),
            pltpu.VMEM((2 * high, slab * rows), BF),
            pltpu.VMEM((slab * rows, LANES + CHUNK), BF),
            pltpu.VMEM((slab, flat, LANES + CHUNK), BF),
            pltpu.VMEM((rows, CHUNK), F32),
            pltpu.VMEM((slab * rows, CHUNK), BF),
            pltpu.VMEM((chunks, slab * rows, CHUNK), BF),
            pltpu.VMEM((chunks, flat, CHUNK), F32),
            pltpu.VMEM((chunks * per + 1, flat, LANES), BF),
            pltpu.VMEM((depth, tile // LANES + 1, flat, LANES), BF),
            pltpu.VMEM((flat, tile + LANES), F32),
            pltpu.VMEM((2, pieces, packed, CHUNK), BF),
            pltpu.VMEM((2, pieces, packed, CHUNK), BF),
            dma((2, chunks)),
            dma((2, chunks + 1)),
            dma((2, chunks + 1)),
            dma((2, chunks)),
            dma((2, chunks)),
            dma((2, chunks)),
            dma((2, chunks)),
            dma((2, chunks)),
            dma((depth, pieces + 1)),
            dma((2, pieces)),
            dma((2, pieces)),
        ],
        compiler_params=pltpu.CompilerParams(
            collective_id=number, has_side_effects=True, vmem_limit_bytes=60 * 2**20
        ),
        name=f"slab_{high}",
    )(*scalars, at, slots, warp, turn, volume)


def swapped(value, axis, mask):
    pairs = [(source, source ^ mask) for source in range(lax.axis_size(axis))]
    return lax.ppermute(value, axis, pairs)


def classes_of(slab):
    top = -(-slab * RIM // GROUP) * GROUP
    rough = {int(slab * f) // GROUP * GROUP for f in (3, 4, 5, 6)}
    return sorted({h for h in rough if h >= 2 * GROUP} | {top})


def per_device(volume, shear_rows, shear_cols, warp_cols, warp_rows):
    channels, slab, rows, cols = volume.shape
    depth = lax.axis_size("depth")
    n_rows = lax.axis_size("rows")

    n_up = jnp.maximum(0, shear_rows + 1)
    n_dn = jnp.maximum(0, 1 - shear_rows)
    end_up = jnp.cumsum(n_up)
    end_dn = jnp.cumsum(n_dn)
    off_up = end_up - n_up
    off_dn = end_dn - n_dn
    need = jnp.maximum(end_up[-1], end_dn[-1]).astype(jnp.int32)
    for other in [swapped(need, "depth", m) for m in range(1, depth)]:
        need = jnp.maximum(need, other)
    row = jnp.arange(EDGE, dtype=jnp.int32)
    at_up = jnp.where(row[None] < n_up[:, None], off_up[:, None] + row[None], -1)
    back = row[None] - (EDGE - n_dn[:, None])
    at_dn = jnp.where(back >= 0, off_dn[:, None] + back, -1)
    at = jnp.stack([at_up, at_dn]).reshape(2, -1)
    y = jnp.arange(rows, dtype=jnp.int32)[None]
    north = jnp.where(y < n_dn[:, None], off_dn[:, None] + y, -1)
    back = y - (rows - n_up[:, None])
    south = jnp.where(back >= 0, off_up[:, None] + back, -1)
    slots = jnp.stack([north, south, jnp.broadcast_to(shear_rows[:, None], north.shape)]).reshape(3, -1)
    row_start = lax.axis_index("rows") * rows
    warp = lax.dynamic_slice_in_dim(warp_cols, row_start, rows, 0).reshape(rows, 1)
    scalars = (shear_rows, shear_cols, off_up, off_dn)

    sizes = classes_of(slab)
    which = sum((need > size).astype(jnp.int32) for size in sizes[:-1])
    branches = [
        functools.partial(slab_stage, size, number + 1, depth, n_rows)
        for number, size in enumerate(sizes)
    ]
    turn = warp_rows.reshape(1, -1)
    return lax.switch(which, branches, volume, scalars, at, slots, warp, turn)


def solution(mesh):
    return jax.shard_map(
        per_device,
        mesh=mesh,
        in_specs=(P(None, "depth", "rows", None), P("depth"), P("depth"), P(), P("depth")),
        out_specs=P(None, "rows", "depth"),
        check_vma=False,
    )
```

```python
import functools

import jax
import jax.numpy as jnp
from jax import lax
from jax.experimental import pallas as pl
from jax.experimental.pallas import tpu as pltpu
from jax.sharding import PartitionSpec as P

SHIFT = 8
RIM = SHIFT + 1
GROUP = 16
EDGE = 16
LANES = 128
LEAD = 16
CHUNK = 512
BLOCK = 8
SLOT = 10
AHEAD = 4
GHOST_LAG = 2
MERGE_LAG = 4
BF = jnp.bfloat16
F32 = jnp.float32
MESH = pl.DeviceIdType.MESH


def weight_of(offset):
    return jnp.where(offset == 0, 0.5, jnp.where(jnp.abs(offset) == 1, 0.25, 0.0)).astype(F32)


def iota(shape, dim):
    return lax.broadcasted_iota(jnp.int32, shape, dim)


def slab_kernel(
    sizes, row_s, col_s, warp_s, turn_ref, vol_hbm,
    out_ref,
    vol, a_send, a_recv, t_send, t_recv, c_send, c_recv, spread, own_w, colour_w, w_col, unpack, collect,
    pick_a, pick_t, band_a, band_c, trans, t_all, ghost, acc, outb, parts, wide_ref, f_send, f_recv,
    load_sem, a_ss, a_rs, t_ss, t_rs, c_ss, c_rs, s_part, r_part, f_ss, f_rs,
):
    depth, n_rows = sizes
    chunks, channels, slab, rows, _ = vol.shape
    colours = channels - 1
    high = a_send.shape[2]
    cols = chunks * CHUNK
    tile = cols // depth
    per = CHUNK // LANES
    per_tile = tile // LANES
    pieces = tile // CHUNK
    flat = channels * rows
    tint = colours * rows
    step = BLOCK * rows
    me = lax.axis_index("depth")
    row = lax.axis_index("rows")
    has = (row > 0, row < n_rows - 1)
    got = (row < n_rows - 1, row > 0)
    target = (jnp.maximum(row - 1, 0), jnp.minimum(row + 1, n_rows - 1))

    def load_alpha(i):
        at = pl.ds(pl.multiple_of(i * CHUNK, CHUNK), CHUNK)
        return pltpu.make_async_copy(vol_hbm.at[colours, :, :, at], vol.at[i, colours], load_sem.at[0, i])

    def load_colour(i):
        at = pl.ds(pl.multiple_of(i * CHUNK, CHUNK), CHUNK)
        return pltpu.make_async_copy(
            vol_hbm.at[pl.ds(0, colours), :, :, at], vol.at[i, pl.ds(0, colours)], load_sem.at[1, i]
        )

    order = [chunks - 1] + list(range(chunks - 1))
    for i in order:
        load_alpha(i).start()
    for i in order:
        load_colour(i).start()

    barrier = pltpu.get_barrier_semaphore()
    for r in (lax.rem(row + 1, n_rows), lax.rem(row + n_rows - 1, n_rows)):
        pl.semaphore_signal(barrier, inc=1, device_id=(me, r), device_id_type=MESH)
    for m in range(1, depth):
        pl.semaphore_signal(barrier, inc=1, device_id=(lax.rem(me + m, depth), row), device_id_type=MESH)
    pl.semaphore_wait(barrier, depth + 1)

    def message(kind, way, i):
        source, dest, ss, rs = kind
        return pltpu.make_async_remote_copy(
            source.at[way, i], dest.at[way, i], ss.at[way, i], rs.at[way, i],
            device_id=(me, target[way]), device_id_type=MESH,
        )

    def lead_message(way):
        part = pl.ds(0, LANES)
        return pltpu.make_async_remote_copy(
            a_send.at[way, chunks, :, part], a_recv.at[way, chunks, :, part],
            a_ss.at[way, chunks], a_rs.at[way, chunks],
            device_id=(me, target[way]), device_id_type=MESH,
        )

    kind_a = (a_send, a_recv, a_ss, a_rs)
    kind_t = (t_send, t_recv, t_ss, t_rs)
    kind_c = (c_send, c_recv, c_ss, c_rs)
    kind_f = (f_send, f_recv, f_ss, f_rs)

    def start(kind, i):
        for way in range(2):
            @pl.when(has[way])
            def _():
                message(kind, way, i).start()

    def arrived(kind, i):
        for way in range(2):
            @pl.when(got[way])
            def _():
                message(kind, way, i).wait_recv()

    def sent(kind, i):
        for way in range(2):
            @pl.when(has[way])
            def _():
                message(kind, way, i).wait_send()

    def counts(k):
        return jnp.maximum(0, row_s[k] + 1), jnp.maximum(0, 1 - row_s[k])

    def tables(k, carry):
        ou, od, at, slots, side = carry
        n_up, n_dn = counts(k)
        u = iota((1, slab * EDGE), 1) - k * EDGE
        v = u - (EDGE - n_dn)
        up = jnp.where((u >= 0) & (u < n_up), ou + u, at[0])
        dn = jnp.where((v >= 0) & (u < EDGE), od + v, at[1])
        u = iota((1, slab * rows), 1) - k * rows
        v = u - (rows - n_up)
        north = jnp.where((u >= 0) & (u < n_dn), od + u, slots[0])
        south = jnp.where((v >= 0) & (u < rows), ou + v, slots[1])
        side = jnp.where((u >= 0) & (u < rows), row_s[k], side)
        return ou + n_up, od + n_dn, (up, dn), (north, south), side

    none = jnp.full((1, slab * EDGE), -1, jnp.int32)
    nowhere = jnp.full((1, slab * rows), -1, jnp.int32)
    zero = jnp.int32(0)
    table = lax.fori_loop(0, slab, tables, (zero, zero, (none, none), (nowhere, nowhere), nowhere))
    _, _, at_rows, slot_rows, shift_of = table

    firsts = (0, rows - EDGE)
    for way in range(2):
        slots = at_rows[way]
        pick_a[way] = (iota((high, slab * EDGE), 0) == slots).astype(F32).astype(BF)

    def pack(i, way, at):
        first = firsts[way]
        source = vol[i, colours, :, first : first + EDGE, at : CHUNK]
        source = source.reshape(slab * EDGE, CHUNK - at)
        return jnp.dot(pick_a[way], source, preferred_element_type=F32).astype(BF)

    load_alpha(chunks - 1).wait()
    for way in range(2):
        a_send[way, chunks, :, :LANES] = pack(chunks - 1, way, CHUNK - LANES)

    @pl.loop(0, chunks)
    def _(i):
        @pl.when(i < chunks - 1)
        def _():
            load_alpha(i).wait()

        for way in range(2):
            a_send[way, i] = pack(i, way, 0)

        @pl.when(i == 0)
        def _():
            for way in range(2):
                @pl.when(has[way])
                def _():
                    lead_message(way).start()

        @pl.when((i > 0) & (i <= AHEAD))
        def _():
            start(kind_a, i - 1)

    for way in range(2):
        @pl.when(jnp.logical_not(got[way]))
        def _():
            a_recv[way] = jnp.zeros(a_recv.shape[1:], BF)
            t_recv[way] = jnp.zeros(t_recv.shape[1:], BF)
            c_recv[way] = jnp.zeros(c_recv.shape[1:], BF)
            f_recv[way] = jnp.zeros(f_recv.shape[1:], BF)

    lane = iota((high, slab * rows), 0)
    for way in range(2):
        slots = slot_rows[way]
        pick_t[way * high : (way + 1) * high] = (lane == slots).astype(F32).astype(BF)
    shape = (2 * rows, slab * rows)
    m = iota(shape, 0)
    j = iota(shape, 1)
    s = shift_of
    e = (j % rows) % SLOT
    side = jnp.where(s > 0, 0, jnp.where(s < 0, 1, jnp.where(e >= SHIFT // 2 + 1, 0, 1)))
    collect[...] = (((m % rows) + rows * (m // rows)) == ((j % rows) + rows * side)).astype(F32).astype(BF)

    def build(k, carry):
        ou, od = carry
        s = row_s[k]
        n_up, n_dn = counts(k)
        mine = pl.ds(pl.multiple_of(k * rows, rows), rows)
        y = iota((rows, high), 0)
        slot = iota((rows, high), 1)
        u = slot - ou
        keep = (u >= 0) & (u < n_up)
        spread[mine, :high] = jnp.where(keep, weight_of(rows + u - y - s), 0.0).astype(BF)
        v = slot - od
        keep = (v >= 0) & (v < n_dn)
        spread[mine, high:] = jnp.where(keep, weight_of(v - n_dn - y - s), 0.0).astype(BF)
        e = jnp.where(y < colours * SLOT, y % SLOT, -1 - 2 * rows)
        e = jnp.where(e > SHIFT, -1 - 2 * rows, e)
        hit = (v == e) & (v < n_dn) & (v >= 0)
        unpack[mine, :high] = hit.astype(F32).astype(BF)
        hit = (u == e - SHIFT + s) & (u < n_up) & (u >= 0)
        unpack[mine, high:] = hit.astype(F32).astype(BF)
        y = iota((rows, step), 0)
        j = iota((rows, step), 1)
        own_w[mine] = jnp.where(
            (j // rows) == lax.rem(k, BLOCK), weight_of((j % rows) - y - s), 0.0
        ).astype(BF)
        m = iota((flat, tint), 0)
        j = iota((flat, tint), 1)
        e = (m - tint) % SLOT
        north = jnp.where(s > 0, 1, jnp.where(s < 0, 0, jnp.where(e >= SHIFT // 2 + 1, 1, 0)))
        y = jnp.where(m < tint, m % rows, jnp.where(north > 0, e - RIM, rows + e))
        c = jnp.where(m < tint, m // rows, (m - tint) // SLOT)
        same = c == (j // rows)
        colour_w[k] = jnp.where(same, weight_of((j % rows) - y - s), 0.0).astype(BF)
        shape = (2 * LANES, LANES)
        m = iota(shape, 0)
        n = iota(shape, 1)
        w = weight_of(m - n - (LANES - LEAD) - col_s[k])
        w_col[0, k] = w.astype(BF)
        w_col[1, k] = jnp.where(jnp.where(m < LANES, 0, 1) == jnp.where(n < LEAD, 0, 1), w, 0.0).astype(BF)
        return ou + n_up, od + n_dn

    lax.fori_loop(0, slab, build, (zero, zero))

    def alpha_rows(i, at, to, width):
        halo = jnp.concatenate([a_recv[way, i, :, :width] for way in range(2)], 0)
        source = i if at == 0 else chunks - 1
        for b in range(slab // BLOCK):
            part = slice(b * step, (b + 1) * step)
            own = vol[source, colours, b * BLOCK : (b + 1) * BLOCK, :, at : at + width]
            own = own.reshape(step, width)
            total = jnp.dot(own_w[part], own, preferred_element_type=F32)
            total = total + jnp.dot(spread[part], halo, preferred_element_type=F32)
            band_a[part, to : to + width] = total.astype(BF)

    def colour_rows(i, k, at, width):
        opacity = vol[i, colours, k, :, at : at + width]
        own = [vol[i, c, k, :, at : at + width] * opacity for c in range(colours)]
        return jnp.dot(colour_w[k], jnp.concatenate(own, 0), preferred_element_type=F32).astype(BF)

    for way in range(2):
        @pl.when(got[way])
        def _():
            lead_message(way).wait_recv()

    alpha_rows(chunks, CHUNK - LANES, CHUNK, LANES)
    load_colour(chunks - 1).wait()

    @pl.loop(0, slab)
    def _(k):
        band_c[k, :, CHUNK:] = colour_rows(chunks - 1, k, CHUNK - LANES, LANES)

    def composite(i):
        arrived(kind_a, i)

        @pl.when(i < chunks - 1)
        def _():
            load_colour(i).wait()

        band_a[:, :LANES] = band_a[:, CHUNK:]
        alpha_rows(i, 0, LANES, CHUNK)
        trans[...] = jnp.ones_like(trans)
        acc[i] = jnp.zeros(acc.shape[1:], F32)
        lead = jnp.where(i == 0, 1, 0)

        @pl.loop(0, slab, unroll=4)
        def _(k):
            band_c[k, :, :LANES] = band_c[k, :, CHUNK:]
            band_c[k, :, LANES:] = colour_rows(i, k, 0, CHUNK)

        @pl.loop(0, slab, unroll=4)
        def _(k):
            mine = pl.ds(pl.multiple_of(k * rows, rows), rows)

            def window(w):
                at = slice(w * LANES, (w + 2) * LANES)
                return [band_a[mine, at], band_c[k, :, at]]

            first = jnp.dot(
                jnp.concatenate(window(0), 0), w_col[lead, k], preferred_element_type=F32
            )
            others = sum([window(w) for w in range(1, per)], [])
            rest = jnp.dot(jnp.concatenate(others, 0), w_col[0, k], preferred_element_type=F32)
            tall = rows + flat
            for w in range(per):
                sheared = first if w == 0 else rest[(w - 1) * tall : w * tall]
                at = slice(w * LANES, (w + 1) * LANES)
                t = trans[:, at]
                for c in range(colours):
                    acc[i, c * rows : (c + 1) * rows, at] += t * sheared[(c + 1) * rows : (c + 2) * rows]
                ghost[i, mine, at] = sheared[flat:].astype(BF)
                t_all[mine, at] = t.astype(BF)
                trans[:, at] = t - t * sheared[:rows]

        acc[i, tint:] = 1.0 - trans[...]
        picked = jnp.dot(pick_t[...], t_all[...], preferred_element_type=F32).astype(BF)
        t_send[0, i] = picked[:high]
        t_send[1, i] = picked[high:]

    def ghosts(i):
        arrived(kind_t, i)
        seen = jnp.concatenate([t_recv[0, i], t_recv[1, i]], 0)
        total = None
        for b in range(slab // BLOCK):
            part = slice(b * step, (b + 1) * step)
            t = jnp.dot(unpack[part], seen, preferred_element_type=F32)
            seen_colour = (t * ghost[i, part].astype(F32)).astype(BF)
            value = jnp.dot(collect[:, part], seen_colour, preferred_element_type=F32)
            total = value if total is None else total + value
        total = total.astype(BF)
        c_send[0, i] = total[:rows]
        c_send[1, i] = total[rows:]

    def merge(i):
        arrived(kind_c, i)
        m = iota((tint, 2 * rows), 0)
        j = iota((tint, 2 * rows), 1)
        e = (j % rows) % SLOT
        y = jnp.where(j < rows, rows - RIM + e, e)
        there = (m // rows == (j % rows) // SLOT) & (m % rows == y) & (e <= SHIFT)
        place = there.astype(F32).astype(BF)
        both = jnp.concatenate([c_recv[0, i], c_recv[1, i]], 0)
        more = jnp.dot(place, both, preferred_element_type=F32)
        image = jnp.concatenate([acc[i, :tint] + more, acc[i, tint:]], 0)
        for w in range(per):
            outb[i * per + w] = image[:, w * LANES : (w + 1) * LANES].astype(BF)

        @pl.when(i == 0)
        def _():
            piece = image[:, :LANES]
            n = iota((flat, LANES), 1)
            outb[chunks * per] = jnp.where(n < LEAD, piece, 0.0).astype(BF)
            outb[0] = jnp.where(n < LEAD, 0.0, piece).astype(BF)

    def part_copy(i, source, count, owner, at, margin):
        return pltpu.make_async_remote_copy(
            outb.at[pl.ds(source, count)],
            parts.at[me, pl.ds(at, count)],
            s_part.at[margin, i],
            r_part.at[me, pieces if margin else lax.rem(i, pieces)],
            device_id=(owner, row),
            device_id_type=MESH,
        )

    def deliver(i, act, keep):
        owner = i // pieces
        at = lax.rem(i, pieces) * per

        @pl.when(owner != me)
        def _():
            act(part_copy(i, i * per, per, owner, at, 0))

        if keep:
            @pl.when(owner == me)
            def _():
                parts[me, pl.ds(at, per)] = outb[pl.ds(i * per, per)]

        margin = lax.rem(i, pieces) == 0
        left = lax.rem(owner + depth - 1, depth)
        source = jnp.where(i == 0, chunks * per, i * per)

        @pl.when(margin & (left != me))
        def _():
            act(part_copy(i, source, 1, left, per_tile, 1))

        if keep:
            @pl.when(margin & (left == me))
            def _():
                parts[me, per_tile] = outb[source]

    @pl.loop(0, chunks + MERGE_LAG)
    def _(i):
        @pl.when(i < chunks)
        def _():
            composite(i)

        @pl.when((i >= GHOST_LAG) & (i < chunks + GHOST_LAG))
        def _():
            ghosts(i - GHOST_LAG)

        @pl.when(i < chunks)
        def _():
            start(kind_t, i)

        @pl.when(i + AHEAD < chunks)
        def _():
            start(kind_a, i + AHEAD)

        @pl.when(i > MERGE_LAG)
        def _():
            deliver(i - MERGE_LAG - 1, lambda copy: copy.start(), True)

        @pl.when(i >= MERGE_LAG)
        def _():
            merge(i - MERGE_LAG)

        @pl.when((i >= GHOST_LAG) & (i < chunks + GHOST_LAG))
        def _():
            start(kind_c, i - GHOST_LAG)

    deliver(jnp.int32(chunks - 1), lambda copy: copy.start(), True)

    for d in range(depth):
        @pl.when(me != d)
        def _():
            for p in range(pieces + 1):
                count = per if p < pieces else 1
                pltpu.make_async_remote_copy(
                    outb.at[pl.ds(0, count)],
                    parts.at[d, pl.ds(p * per, count)],
                    s_part.at[0, 0],
                    r_part.at[d, p],
                    device_id=(me, row),
                    device_id_type=MESH,
                ).wait_recv()

    for w in range(per_tile + 1):
        image = parts[0, w].astype(F32)
        image = image.reshape(channels, rows, LANES)
        for d in range(1, depth):
            back = parts[d, w].astype(F32).reshape(channels, rows, LANES)
            image = image + (1.0 - image[channels - 1 :]) * back
        wide_ref[:, w * LANES : (w + 1) * LANES] = image.reshape(flat, LANES)

    amount = jnp.zeros((rows, LANES), jnp.int32)
    for y in range(rows):
        amount = jnp.where(iota((rows, LANES), 0) == y, warp_s[row * rows + y] + SHIFT, amount)
    amount = jnp.concatenate([amount] * ((CHUNK + LANES) // LANES), 1)
    packed = f_send.shape[2]
    m = iota((packed, flat), 0)
    j = iota((packed, flat), 1)
    picks = []
    for first in (0, rows - RIM):
        there = (m // RIM == j // rows) & (m % RIM + first == j % rows)
        picks.append(there.astype(F32).astype(BF))
    width = CHUNK + LANES
    for h in range(pieces):
        lines = []
        for c in range(channels):
            line = wide_ref[c * rows : (c + 1) * rows, h * CHUNK : h * CHUNK + width]
            line = 0.5 * line + 0.25 * (pltpu.roll(line, 1, 1) + pltpu.roll(line, width - 1, 1))
            line = pltpu.roll(line, width - (LEAD - SHIFT), 1)
            for bit in (1, 2, 4, 8, 16):
                line = jnp.where((amount & bit) != 0, pltpu.roll(line, width - bit, 1), line)
            lines.append(line[:, :CHUNK])
        across = jnp.concatenate(lines, 0)
        wide_ref[:, h * CHUNK : (h + 1) * CHUNK] = across
        across = across.astype(BF)
        for way in range(2):
            f_send[way, h] = jnp.dot(picks[way], across, preferred_element_type=F32).astype(BF)
        if h > 0:
            start(kind_f, h - 1)
    start(kind_f, pieces - 1)

    half = rows // 2
    m = iota((flat, 2 * packed), 0)
    j = iota((flat, 2 * packed), 1)
    a = m % rows
    e = jnp.where(j < packed, a - half + RIM, a - half)
    slot = jnp.where(j < packed, j, j - packed)
    wanted = jnp.where(a < half, jnp.where(j < packed, e, -1), jnp.where(j < packed, -1, e))
    place = (slot // RIM == m // rows) & (slot % RIM == wanted)
    place = place.astype(F32).astype(BF)
    for h in range(pieces):
        arrived(kind_f, h)
        at = slice(h * CHUNK, (h + 1) * CHUNK)
        rim = jnp.concatenate([f_recv[1, h], f_recv[0, h]], 0)
        rim = jnp.dot(place, rim, preferred_element_type=F32)
        turn = turn_ref[:, at] + SHIFT
        for c in range(channels):
            low = rim[c * rows : c * rows + half]
            high_rows = rim[c * rows + half : (c + 1) * rows]
            ext = jnp.concatenate([low, wide_ref[c * rows : (c + 1) * rows, at], high_rows], 0)
            tall = ext.shape[0]
            ext = 0.5 * ext + 0.25 * (pltpu.roll(ext, 1, 0) + pltpu.roll(ext, tall - 1, 0))
            line = ext[half - SHIFT :]
            keep = rows + 2 * SHIFT
            line = jnp.where((turn & 8) != 0, line[8 : 8 + keep], line[:keep])
            far = jnp.concatenate([line[16 : 16 + rows], line[16 + rows - 8 : 16 + rows]], 0)
            line = jnp.where((turn & 16) != 0, far, line[: rows + 8])
            tall = rows + 8
            for bit in (4, 2, 1):
                line = jnp.where((turn & bit) != 0, pltpu.roll(line, tall - bit, 0), line)
            out_ref[c, :, at] = line[:rows]

    for way in range(2):
        @pl.when(has[way])
        def _():
            lead_message(way).wait_send()

    @pl.loop(0, chunks)
    def _(i):
        for kind in (kind_a, kind_t, kind_c):
            sent(kind, i)
        deliver(i, lambda copy: copy.wait_send(), False)

    for h in range(pieces):
        sent(kind_f, h)


def slab_stage(high, number, depth, n_rows, volume, scalars, turn):
    channels, slab, rows, cols = volume.shape
    chunks = cols // CHUNK
    per = CHUNK // LANES
    tile = cols // depth
    flat = channels * rows
    tint = flat - rows
    pieces = tile // CHUNK
    smem = pl.BlockSpec(memory_space=pltpu.SMEM)
    vmem = pl.BlockSpec(memory_space=pltpu.VMEM)
    packed = -(-channels * RIM // EDGE) * EDGE
    dma = pltpu.SemaphoreType.DMA
    return pl.pallas_call(
        functools.partial(slab_kernel, (depth, n_rows)),
        in_specs=[smem] * 3 + [vmem] + [pl.BlockSpec(memory_space=pl.ANY)],
        out_specs=vmem,
        out_shape=jax.ShapeDtypeStruct((channels, rows, tile), F32),
        scratch_shapes=[
            pltpu.VMEM((chunks, channels, slab, rows, CHUNK), BF),
            pltpu.VMEM((2, chunks + 1, high, CHUNK), BF),
            pltpu.VMEM((2, chunks + 1, high, CHUNK), BF),
            pltpu.VMEM((2, chunks, high, CHUNK), BF),
            pltpu.VMEM((2, chunks, high, CHUNK), BF),
            pltpu.VMEM((2, chunks, rows, CHUNK), BF),
            pltpu.VMEM((2, chunks, rows, CHUNK), BF),
            pltpu.VMEM((slab * rows, 2 * high), BF),
            pltpu.VMEM((slab * rows, BLOCK * rows), BF),
            pltpu.VMEM((slab, flat, tint), BF),
            pltpu.VMEM((2, slab, 2 * LANES, LANES), BF),
            pltpu.VMEM((slab * rows, 2 * high), BF),
            pltpu.VMEM((2 * rows, slab * rows), BF),
            pltpu.VMEM((2, high, slab * EDGE), BF),
            pltpu.VMEM((2 * high, slab * rows), BF),
            pltpu.VMEM((slab * rows, LANES + CHUNK), BF),
            pltpu.VMEM((slab, flat, LANES + CHUNK), BF),
            pltpu.VMEM((rows, CHUNK), F32),
            pltpu.VMEM((slab * rows, CHUNK), BF),
            pltpu.VMEM((chunks, slab * rows, CHUNK), BF),
            pltpu.VMEM((chunks, flat, CHUNK), F32),
            pltpu.VMEM((chunks * per + 1, flat, LANES), BF),
            pltpu.VMEM((depth, tile // LANES + 1, flat, LANES), BF),
            pltpu.VMEM((flat, tile + LANES), F32),
            pltpu.VMEM((2, pieces, packed, CHUNK), BF),
            pltpu.VMEM((2, pieces, packed, CHUNK), BF),
            dma((2, chunks)),
            dma((2, chunks + 1)),
            dma((2, chunks + 1)),
            dma((2, chunks)),
            dma((2, chunks)),
            dma((2, chunks)),
            dma((2, chunks)),
            dma((2, chunks)),
            dma((depth, pieces + 1)),
            dma((2, pieces)),
            dma((2, pieces)),
        ],
        compiler_params=pltpu.CompilerParams(
            collective_id=number, has_side_effects=True, vmem_limit_bytes=60 * 2**20
        ),
        name=f"slab_{high}",
    )(*scalars, turn, volume)


def swapped(value, axis, mask):
    pairs = [(source, source ^ mask) for source in range(lax.axis_size(axis))]
    return lax.ppermute(value, axis, pairs)


def classes_of(slab):
    top = -(-slab * RIM // GROUP) * GROUP
    rough = {int(slab * f) // GROUP * GROUP for f in (3, 4, 5, 6)}
    return sorted({h for h in rough if h >= 2 * GROUP} | {top})


def per_device(volume, shear_rows, shear_cols, warp_cols, warp_rows):
    channels, slab, rows, cols = volume.shape
    depth = lax.axis_size("depth")
    n_rows = lax.axis_size("rows")

    n_up = jnp.maximum(0, shear_rows + 1)
    n_dn = jnp.maximum(0, 1 - shear_rows)
    need = jnp.maximum(jnp.sum(n_up), jnp.sum(n_dn)).astype(jnp.int32)
    for other in [swapped(need, "depth", m) for m in range(1, depth)]:
        need = jnp.maximum(need, other)
    scalars = (shear_rows, shear_cols, warp_cols)
    sizes = classes_of(slab)
    which = sum((need > size).astype(jnp.int32) for size in sizes[:-1])
    branches = [
        functools.partial(slab_stage, size, number + 1, depth, n_rows)
        for number, size in enumerate(sizes)
    ]
    turn = warp_rows.reshape(1, -1)
    return lax.switch(which, branches, volume, scalars, turn)


def solution(mesh):
    return jax.shard_map(
        per_device,
        mesh=mesh,
        in_specs=(P(None, "depth", "rows", None), P("depth"), P("depth"), P(), P("depth")),
        out_specs=P(None, "rows", "depth"),
        check_vma=False,
    )
```

```python
import functools

import jax
import jax.numpy as jnp
from jax import lax
from jax.experimental import pallas as pl
from jax.experimental.pallas import tpu as pltpu
from jax.sharding import PartitionSpec as P

SHIFT = 8
RIM = SHIFT + 1
GROUP = 8
EDGE = 16
LANES = 128
LEAD = 16
CHUNK = 512
BLOCK = 8
SLOT = 10
AHEAD = 4
GHOST_LAG = 2
MERGE_LAG = 4
BF = jnp.bfloat16
F32 = jnp.float32
MESH = pl.DeviceIdType.MESH


def weight_of(offset):
    return jnp.where(offset == 0, 0.5, jnp.where(jnp.abs(offset) == 1, 0.25, 0.0)).astype(F32)


def iota(shape, dim):
    return lax.broadcasted_iota(jnp.int32, shape, dim)


def slab_kernel(
    sizes, row_s, col_s, warp_s, turn_ref, vol_hbm,
    out_ref,
    vol, a_send, a_recv, t_send, t_recv, c_send, c_recv, spread, own_w, colour_w, w_col, unpack, collect,
    pick_a, pick_t, band_a, band_c, trans, t_all, ghost, acc, outb, parts, wide_ref, f_send, f_recv,
    load_sem, a_ss, a_rs, t_ss, t_rs, c_ss, c_rs, s_part, r_part, f_ss, f_rs,
):
    depth, n_rows, wire = sizes
    chunks, channels, slab, rows, _ = vol.shape
    colours = channels - 1
    high = a_send.shape[2]
    cols = chunks * CHUNK
    tile = cols // depth
    per = CHUNK // LANES
    per_tile = tile // LANES
    pieces = tile // CHUNK
    flat = channels * rows
    tint = colours * rows
    step = BLOCK * rows
    me = lax.axis_index("depth")
    row = lax.axis_index("rows")
    has = (row > 0, row < n_rows - 1)
    got = (row < n_rows - 1, row > 0)
    target = (jnp.maximum(row - 1, 0), jnp.minimum(row + 1, n_rows - 1))

    def load_alpha(i):
        at = pl.ds(pl.multiple_of(i * CHUNK, CHUNK), CHUNK)
        return pltpu.make_async_copy(vol_hbm.at[colours, :, :, at], vol.at[i, colours], load_sem.at[0, i])

    def load_colour(i):
        at = pl.ds(pl.multiple_of(i * CHUNK, CHUNK), CHUNK)
        return pltpu.make_async_copy(
            vol_hbm.at[pl.ds(0, colours), :, :, at], vol.at[i, pl.ds(0, colours)], load_sem.at[1, i]
        )

    order = [chunks - 1] + list(range(chunks - 1))
    for i in order:
        load_alpha(i).start()
    for i in order:
        load_colour(i).start()

    if wire < high:
        for ref in (a_recv, t_recv):
            ref[:, :, high - EDGE :] = jnp.zeros(ref.shape[:2] + (EDGE, CHUNK), BF)

    barrier = pltpu.get_barrier_semaphore()
    for r in (lax.rem(row + 1, n_rows), lax.rem(row + n_rows - 1, n_rows)):
        pl.semaphore_signal(barrier, inc=1, device_id=(me, r), device_id_type=MESH)
    for m in range(1, depth):
        pl.semaphore_signal(barrier, inc=1, device_id=(lax.rem(me + m, depth), row), device_id_type=MESH)
    pl.semaphore_wait(barrier, depth + 1)

    def message(kind, way, i):
        source, dest, ss, rs = kind
        part = pl.ds(0, wire if source.shape[2] == high else source.shape[2])
        return pltpu.make_async_remote_copy(
            source.at[way, i, part], dest.at[way, i, part], ss.at[way, i], rs.at[way, i],
            device_id=(me, target[way]), device_id_type=MESH,
        )

    def lead_message(way):
        part = pl.ds(0, LANES)
        return pltpu.make_async_remote_copy(
            a_send.at[way, chunks, pl.ds(0, wire), part], a_recv.at[way, chunks, pl.ds(0, wire), part],
            a_ss.at[way, chunks], a_rs.at[way, chunks],
            device_id=(me, target[way]), device_id_type=MESH,
        )

    kind_a = (a_send, a_recv, a_ss, a_rs)
    kind_t = (t_send, t_recv, t_ss, t_rs)
    kind_c = (c_send, c_recv, c_ss, c_rs)
    kind_f = (f_send, f_recv, f_ss, f_rs)

    def start(kind, i):
        for way in range(2):
            @pl.when(has[way])
            def _():
                message(kind, way, i).start()

    def arrived(kind, i):
        for way in range(2):
            @pl.when(got[way])
            def _():
                message(kind, way, i).wait_recv()

    def sent(kind, i):
        for way in range(2):
            @pl.when(has[way])
            def _():
                message(kind, way, i).wait_send()

    def counts(k):
        return jnp.maximum(0, row_s[k] + 1), jnp.maximum(0, 1 - row_s[k])

    def tables(k, carry):
        ou, od, at, slots, side = carry
        n_up, n_dn = counts(k)
        u = iota((1, slab * EDGE), 1) - k * EDGE
        v = u - (EDGE - n_dn)
        up = jnp.where((u >= 0) & (u < n_up), ou + u, at[0])
        dn = jnp.where((v >= 0) & (u < EDGE), od + v, at[1])
        u = iota((1, slab * rows), 1) - k * rows
        v = u - (rows - n_up)
        north = jnp.where((u >= 0) & (u < n_dn), od + u, slots[0])
        south = jnp.where((v >= 0) & (u < rows), ou + v, slots[1])
        side = jnp.where((u >= 0) & (u < rows), row_s[k], side)
        return ou + n_up, od + n_dn, (up, dn), (north, south), side

    none = jnp.full((1, slab * EDGE), -1, jnp.int32)
    nowhere = jnp.full((1, slab * rows), -1, jnp.int32)
    zero = jnp.int32(0)
    table = lax.fori_loop(0, slab, tables, (zero, zero, (none, none), (nowhere, nowhere), nowhere))
    _, _, at_rows, slot_rows, shift_of = table

    firsts = (0, rows - EDGE)
    for way in range(2):
        slots = at_rows[way]
        pick_a[way] = (iota((high, slab * EDGE), 0) == slots).astype(F32).astype(BF)

    def pack(i, way, at):
        first = firsts[way]
        source = vol[i, colours, :, first : first + EDGE, at : CHUNK]
        source = source.reshape(slab * EDGE, CHUNK - at)
        return jnp.dot(pick_a[way], source, preferred_element_type=F32).astype(BF)

    load_alpha(chunks - 1).wait()
    for way in range(2):
        a_send[way, chunks, :, :LANES] = pack(chunks - 1, way, CHUNK - LANES)

    @pl.loop(0, chunks)
    def _(i):
        @pl.when(i < chunks - 1)
        def _():
            load_alpha(i).wait()

        for way in range(2):
            a_send[way, i] = pack(i, way, 0)

        @pl.when(i == 0)
        def _():
            for way in range(2):
                @pl.when(has[way])
                def _():
                    lead_message(way).start()

        @pl.when((i > 0) & (i <= AHEAD))
        def _():
            start(kind_a, i - 1)

    for way in range(2):
        @pl.when(jnp.logical_not(got[way]))
        def _():
            a_recv[way] = jnp.zeros(a_recv.shape[1:], BF)
            t_recv[way] = jnp.zeros(t_recv.shape[1:], BF)
            c_recv[way] = jnp.zeros(c_recv.shape[1:], BF)
            f_recv[way] = jnp.zeros(f_recv.shape[1:], BF)

    lane = iota((high, slab * rows), 0)
    for way in range(2):
        slots = slot_rows[way]
        pick_t[way * high : (way + 1) * high] = (lane == slots).astype(F32).astype(BF)
    shape = (2 * rows, slab * rows)
    m = iota(shape, 0)
    j = iota(shape, 1)
    s = shift_of
    e = (j % rows) % SLOT
    side = jnp.where(s > 0, 0, jnp.where(s < 0, 1, jnp.where(e >= SHIFT // 2 + 1, 0, 1)))
    collect[...] = (((m % rows) + rows * (m // rows)) == ((j % rows) + rows * side)).astype(F32).astype(BF)

    def build(k, carry):
        ou, od = carry
        s = row_s[k]
        n_up, n_dn = counts(k)
        mine = pl.ds(pl.multiple_of(k * rows, rows), rows)
        y = iota((rows, high), 0)
        slot = iota((rows, high), 1)
        u = slot - ou
        keep = (u >= 0) & (u < n_up)
        spread[mine, :high] = jnp.where(keep, weight_of(rows + u - y - s), 0.0).astype(BF)
        v = slot - od
        keep = (v >= 0) & (v < n_dn)
        spread[mine, high:] = jnp.where(keep, weight_of(v - n_dn - y - s), 0.0).astype(BF)
        e = jnp.where(y < colours * SLOT, y % SLOT, -1 - 2 * rows)
        e = jnp.where(e > SHIFT, -1 - 2 * rows, e)
        hit = (v == e) & (v < n_dn) & (v >= 0)
        unpack[mine, :high] = hit.astype(F32).astype(BF)
        hit = (u == e - SHIFT + s) & (u < n_up) & (u >= 0)
        unpack[mine, high:] = hit.astype(F32).astype(BF)
        y = iota((rows, step), 0)
        j = iota((rows, step), 1)
        own_w[mine] = jnp.where(
            (j // rows) == lax.rem(k, BLOCK), weight_of((j % rows) - y - s), 0.0
        ).astype(BF)
        m = iota((flat, tint), 0)
        j = iota((flat, tint), 1)
        e = (m - tint) % SLOT
        north = jnp.where(s > 0, 1, jnp.where(s < 0, 0, jnp.where(e >= SHIFT // 2 + 1, 1, 0)))
        y = jnp.where(m < tint, m % rows, jnp.where(north > 0, e - RIM, rows + e))
        c = jnp.where(m < tint, m // rows, (m - tint) // SLOT)
        same = c == (j // rows)
        colour_w[k] = jnp.where(same, weight_of((j % rows) - y - s), 0.0).astype(BF)
        shape = (2 * LANES, LANES)
        m = iota(shape, 0)
        n = iota(shape, 1)
        w = weight_of(m - n - (LANES - LEAD) - col_s[k])
        w_col[0, k] = w.astype(BF)
        w_col[1, k] = jnp.where(jnp.where(m < LANES, 0, 1) == jnp.where(n < LEAD, 0, 1), w, 0.0).astype(BF)
        return ou + n_up, od + n_dn

    lax.fori_loop(0, slab, build, (zero, zero))

    def alpha_rows(i, at, to, width):
        halo = jnp.concatenate([a_recv[way, i, :, :width] for way in range(2)], 0)
        source = i if at == 0 else chunks - 1
        for b in range(slab // BLOCK):
            part = slice(b * step, (b + 1) * step)
            own = vol[source, colours, b * BLOCK : (b + 1) * BLOCK, :, at : at + width]
            own = own.reshape(step, width)
            total = jnp.dot(own_w[part], own, preferred_element_type=F32)
            total = total + jnp.dot(spread[part], halo, preferred_element_type=F32)
            band_a[part, to : to + width] = total.astype(BF)

    def colour_rows(i, k, at, width):
        opacity = vol[i, colours, k, :, at : at + width]
        own = [vol[i, c, k, :, at : at + width] * opacity for c in range(colours)]
        return jnp.dot(colour_w[k], jnp.concatenate(own, 0), preferred_element_type=F32).astype(BF)

    for way in range(2):
        @pl.when(got[way])
        def _():
            lead_message(way).wait_recv()

    alpha_rows(chunks, CHUNK - LANES, CHUNK, LANES)
    load_colour(chunks - 1).wait()

    @pl.loop(0, slab)
    def _(k):
        band_c[k, :, CHUNK:] = colour_rows(chunks - 1, k, CHUNK - LANES, LANES)

    def composite(i):
        arrived(kind_a, i)

        @pl.when(i < chunks - 1)
        def _():
            load_colour(i).wait()

        band_a[:, :LANES] = band_a[:, CHUNK:]
        alpha_rows(i, 0, LANES, CHUNK)
        trans[...] = jnp.ones_like(trans)
        acc[i] = jnp.zeros(acc.shape[1:], F32)
        lead = jnp.where(i == 0, 1, 0)

        @pl.loop(0, slab, unroll=4)
        def _(k):
            band_c[k, :, :LANES] = band_c[k, :, CHUNK:]
            band_c[k, :, LANES:] = colour_rows(i, k, 0, CHUNK)

        @pl.loop(0, slab, unroll=4)
        def _(k):
            mine = pl.ds(pl.multiple_of(k * rows, rows), rows)

            def window(w):
                at = slice(w * LANES, (w + 2) * LANES)
                return [band_a[mine, at], band_c[k, :, at]]

            first = jnp.dot(
                jnp.concatenate(window(0), 0), w_col[lead, k], preferred_element_type=F32
            )
            others = sum([window(w) for w in range(1, per)], [])
            rest = jnp.dot(jnp.concatenate(others, 0), w_col[0, k], preferred_element_type=F32)
            tall = rows + flat
            for w in range(per):
                sheared = first if w == 0 else rest[(w - 1) * tall : w * tall]
                at = slice(w * LANES, (w + 1) * LANES)
                t = trans[:, at]
                for c in range(colours):
                    acc[i, c * rows : (c + 1) * rows, at] += t * sheared[(c + 1) * rows : (c + 2) * rows]
                ghost[i, mine, at] = sheared[flat:].astype(BF)
                t_all[mine, at] = t.astype(BF)
                trans[:, at] = t - t * sheared[:rows]

        acc[i, tint:] = 1.0 - trans[...]
        picked = jnp.dot(pick_t[...], t_all[...], preferred_element_type=F32).astype(BF)
        t_send[0, i] = picked[:high]
        t_send[1, i] = picked[high:]

    def ghosts(i):
        arrived(kind_t, i)
        seen = jnp.concatenate([t_recv[0, i], t_recv[1, i]], 0)
        total = None
        for b in range(slab // BLOCK):
            part = slice(b * step, (b + 1) * step)
            t = jnp.dot(unpack[part], seen, preferred_element_type=F32)
            seen_colour = (t * ghost[i, part].astype(F32)).astype(BF)
            value = jnp.dot(collect[:, part], seen_colour, preferred_element_type=F32)
            total = value if total is None else total + value
        total = total.astype(BF)
        c_send[0, i] = total[:rows]
        c_send[1, i] = total[rows:]

    def merge(i):
        arrived(kind_c, i)
        m = iota((tint, 2 * rows), 0)
        j = iota((tint, 2 * rows), 1)
        e = (j % rows) % SLOT
        y = jnp.where(j < rows, rows - RIM + e, e)
        there = (m // rows == (j % rows) // SLOT) & (m % rows == y) & (e <= SHIFT)
        place = there.astype(F32).astype(BF)
        both = jnp.concatenate([c_recv[0, i], c_recv[1, i]], 0)
        more = jnp.dot(place, both, preferred_element_type=F32)
        image = jnp.concatenate([acc[i, :tint] + more, acc[i, tint:]], 0)
        for w in range(per):
            outb[i * per + w] = image[:, w * LANES : (w + 1) * LANES].astype(BF)

        @pl.when(i == 0)
        def _():
            piece = image[:, :LANES]
            n = iota((flat, LANES), 1)
            outb[chunks * per] = jnp.where(n < LEAD, piece, 0.0).astype(BF)
            outb[0] = jnp.where(n < LEAD, 0.0, piece).astype(BF)

    def part_copy(i, source, count, owner, at, margin):
        return pltpu.make_async_remote_copy(
            outb.at[pl.ds(source, count)],
            parts.at[me, pl.ds(at, count)],
            s_part.at[margin, i],
            r_part.at[me, pieces if margin else lax.rem(i, pieces)],
            device_id=(owner, row),
            device_id_type=MESH,
        )

    def deliver(i, act, keep):
        owner = i // pieces
        at = lax.rem(i, pieces) * per

        @pl.when(owner != me)
        def _():
            act(part_copy(i, i * per, per, owner, at, 0))

        if keep:
            @pl.when(owner == me)
            def _():
                parts[me, pl.ds(at, per)] = outb[pl.ds(i * per, per)]

        margin = lax.rem(i, pieces) == 0
        left = lax.rem(owner + depth - 1, depth)
        source = jnp.where(i == 0, chunks * per, i * per)

        @pl.when(margin & (left != me))
        def _():
            act(part_copy(i, source, 1, left, per_tile, 1))

        if keep:
            @pl.when(margin & (left == me))
            def _():
                parts[me, per_tile] = outb[source]

    @pl.loop(0, chunks + MERGE_LAG)
    def _(i):
        @pl.when(i < chunks)
        def _():
            composite(i)

        @pl.when((i >= GHOST_LAG) & (i < chunks + GHOST_LAG))
        def _():
            ghosts(i - GHOST_LAG)

        @pl.when(i < chunks)
        def _():
            start(kind_t, i)

        @pl.when(i + AHEAD < chunks)
        def _():
            start(kind_a, i + AHEAD)

        @pl.when(i > MERGE_LAG)
        def _():
            deliver(i - MERGE_LAG - 1, lambda copy: copy.start(), True)

        @pl.when(i >= MERGE_LAG)
        def _():
            merge(i - MERGE_LAG)

        @pl.when((i >= GHOST_LAG) & (i < chunks + GHOST_LAG))
        def _():
            start(kind_c, i - GHOST_LAG)

    deliver(jnp.int32(chunks - 1), lambda copy: copy.start(), True)

    for d in range(depth):
        @pl.when(me != d)
        def _():
            for p in range(pieces + 1):
                count = per if p < pieces else 1
                pltpu.make_async_remote_copy(
                    outb.at[pl.ds(0, count)],
                    parts.at[d, pl.ds(p * per, count)],
                    s_part.at[0, 0],
                    r_part.at[d, p],
                    device_id=(me, row),
                    device_id_type=MESH,
                ).wait_recv()

    for w in range(per_tile + 1):
        image = parts[0, w].astype(F32)
        image = image.reshape(channels, rows, LANES)
        for d in range(1, depth):
            back = parts[d, w].astype(F32).reshape(channels, rows, LANES)
            image = image + (1.0 - image[channels - 1 :]) * back
        wide_ref[:, w * LANES : (w + 1) * LANES] = image.reshape(flat, LANES)

    amount = jnp.zeros((rows, LANES), jnp.int32)
    for y in range(rows):
        amount = jnp.where(iota((rows, LANES), 0) == y, warp_s[row * rows + y] + SHIFT, amount)
    amount = jnp.concatenate([amount] * ((CHUNK + LANES) // LANES), 1)
    packed = f_send.shape[2]
    m = iota((packed, flat), 0)
    j = iota((packed, flat), 1)
    picks = []
    for first in (0, rows - RIM):
        there = (m // RIM == j // rows) & (m % RIM + first == j % rows)
        picks.append(there.astype(F32).astype(BF))
    width = CHUNK + LANES
    for h in range(pieces):
        lines = []
        for c in range(channels):
            line = wide_ref[c * rows : (c + 1) * rows, h * CHUNK : h * CHUNK + width]
            line = 0.5 * line + 0.25 * (pltpu.roll(line, 1, 1) + pltpu.roll(line, width - 1, 1))
            line = pltpu.roll(line, width - (LEAD - SHIFT), 1)
            for bit in (1, 2, 4, 8, 16):
                line = jnp.where((amount & bit) != 0, pltpu.roll(line, width - bit, 1), line)
            lines.append(line[:, :CHUNK])
        across = jnp.concatenate(lines, 0)
        wide_ref[:, h * CHUNK : (h + 1) * CHUNK] = across
        across = across.astype(BF)
        for way in range(2):
            f_send[way, h] = jnp.dot(picks[way], across, preferred_element_type=F32).astype(BF)
        if h > 0:
            start(kind_f, h - 1)
    start(kind_f, pieces - 1)

    half = rows // 2
    m = iota((flat, 2 * packed), 0)
    j = iota((flat, 2 * packed), 1)
    a = m % rows
    e = jnp.where(j < packed, a - half + RIM, a - half)
    slot = jnp.where(j < packed, j, j - packed)
    wanted = jnp.where(a < half, jnp.where(j < packed, e, -1), jnp.where(j < packed, -1, e))
    place = (slot // RIM == m // rows) & (slot % RIM == wanted)
    place = place.astype(F32).astype(BF)
    for h in range(pieces):
        arrived(kind_f, h)
        at = slice(h * CHUNK, (h + 1) * CHUNK)
        rim = jnp.concatenate([f_recv[1, h], f_recv[0, h]], 0)
        rim = jnp.dot(place, rim, preferred_element_type=F32)
        turn = turn_ref[:, at] + SHIFT
        for c in range(channels):
            low = rim[c * rows : c * rows + half]
            high_rows = rim[c * rows + half : (c + 1) * rows]
            ext = jnp.concatenate([low, wide_ref[c * rows : (c + 1) * rows, at], high_rows], 0)
            tall = ext.shape[0]
            ext = 0.5 * ext + 0.25 * (pltpu.roll(ext, 1, 0) + pltpu.roll(ext, tall - 1, 0))
            line = ext[half - SHIFT :]
            keep = rows + 2 * SHIFT
            line = jnp.where((turn & 8) != 0, line[8 : 8 + keep], line[:keep])
            far = jnp.concatenate([line[16 : 16 + rows], line[16 + rows - 8 : 16 + rows]], 0)
            line = jnp.where((turn & 16) != 0, far, line[: rows + 8])
            tall = rows + 8
            for bit in (4, 2, 1):
                line = jnp.where((turn & bit) != 0, pltpu.roll(line, tall - bit, 0), line)
            out_ref[c, :, at] = line[:rows]

    for way in range(2):
        @pl.when(has[way])
        def _():
            lead_message(way).wait_send()

    @pl.loop(0, chunks)
    def _(i):
        for kind in (kind_a, kind_t, kind_c):
            sent(kind, i)
        deliver(i, lambda copy: copy.wait_send(), False)

    for h in range(pieces):
        sent(kind_f, h)


def slab_stage(wire, number, depth, n_rows, volume, scalars, turn):
    channels, slab, rows, cols = volume.shape
    chunks = cols // CHUNK
    high = -(-wire // EDGE) * EDGE
    per = CHUNK // LANES
    tile = cols // depth
    flat = channels * rows
    tint = flat - rows
    pieces = tile // CHUNK
    smem = pl.BlockSpec(memory_space=pltpu.SMEM)
    vmem = pl.BlockSpec(memory_space=pltpu.VMEM)
    packed = -(-channels * RIM // EDGE) * EDGE
    dma = pltpu.SemaphoreType.DMA
    return pl.pallas_call(
        functools.partial(slab_kernel, (depth, n_rows, wire)),
        in_specs=[smem] * 3 + [vmem] + [pl.BlockSpec(memory_space=pl.ANY)],
        out_specs=vmem,
        out_shape=jax.ShapeDtypeStruct((channels, rows, tile), F32),
        scratch_shapes=[
            pltpu.VMEM((chunks, channels, slab, rows, CHUNK), BF),
            pltpu.VMEM((2, chunks + 1, high, CHUNK), BF),
            pltpu.VMEM((2, chunks + 1, high, CHUNK), BF),
            pltpu.VMEM((2, chunks, high, CHUNK), BF),
            pltpu.VMEM((2, chunks, high, CHUNK), BF),
            pltpu.VMEM((2, chunks, rows, CHUNK), BF),
            pltpu.VMEM((2, chunks, rows, CHUNK), BF),
            pltpu.VMEM((slab * rows, 2 * high), BF),
            pltpu.VMEM((slab * rows, BLOCK * rows), BF),
            pltpu.VMEM((slab, flat, tint), BF),
            pltpu.VMEM((2, slab, 2 * LANES, LANES), BF),
            pltpu.VMEM((slab * rows, 2 * high), BF),
            pltpu.VMEM((2 * rows, slab * rows), BF),
            pltpu.VMEM((2, high, slab * EDGE), BF),
            pltpu.VMEM((2 * high, slab * rows), BF),
            pltpu.VMEM((slab * rows, LANES + CHUNK), BF),
            pltpu.VMEM((slab, flat, LANES + CHUNK), BF),
            pltpu.VMEM((rows, CHUNK), F32),
            pltpu.VMEM((slab * rows, CHUNK), BF),
            pltpu.VMEM((chunks, slab * rows, CHUNK), BF),
            pltpu.VMEM((chunks, flat, CHUNK), F32),
            pltpu.VMEM((chunks * per + 1, flat, LANES), BF),
            pltpu.VMEM((depth, tile // LANES + 1, flat, LANES), BF),
            pltpu.VMEM((flat, tile + LANES), F32),
            pltpu.VMEM((2, pieces, packed, CHUNK), BF),
            pltpu.VMEM((2, pieces, packed, CHUNK), BF),
            dma((2, chunks)),
            dma((2, chunks + 1)),
            dma((2, chunks + 1)),
            dma((2, chunks)),
            dma((2, chunks)),
            dma((2, chunks)),
            dma((2, chunks)),
            dma((2, chunks)),
            dma((depth, pieces + 1)),
            dma((2, pieces)),
            dma((2, pieces)),
        ],
        compiler_params=pltpu.CompilerParams(
            collective_id=number, has_side_effects=True, vmem_limit_bytes=60 * 2**20
        ),
        name=f"slab_{wire}",
    )(*scalars, turn, volume)


def class_kernel(sizes, depth, mine_ref, out_ref, seen, ss, rs):
    me = lax.axis_index("depth")
    row = lax.axis_index("rows")
    barrier = pltpu.get_barrier_semaphore()
    for m in range(1, depth):
        pl.semaphore_signal(barrier, inc=1, device_id=(lax.rem(me + m, depth), row), device_id_type=MESH)
    seen[me] = mine_ref[...]
    pl.semaphore_wait(barrier, depth - 1)

    def swap(m):
        return pltpu.make_async_remote_copy(
            mine_ref, seen.at[me], ss.at[m], rs.at[m],
            device_id=(lax.rem(me + m, depth), row), device_id_type=MESH,
        )

    for m in range(1, depth):
        swap(m).start()
    for m in range(1, depth):
        swap(m).wait_recv()
    which = jnp.zeros((1, 1), F32)
    need = jnp.zeros((1, 1), F32)
    for d in range(depth):
        s = seen[d].astype(F32)
        for n in (s + 1.0, 1.0 - s):
            need = jnp.maximum(need, jnp.sum(jnp.maximum(n, 0.0), axis=1, keepdims=True))
    for size in sizes[:-1]:
        which = which + jnp.where(need > size, 1.0, 0.0)
    out_ref[0] = jnp.sum(which).astype(jnp.int32)
    for m in range(1, depth):
        swap(m).wait_send()


def class_of(sizes, depth, shear_rows):
    slab = shear_rows.shape[0]
    return pl.pallas_call(
        functools.partial(class_kernel, sizes, depth),
        in_specs=[pl.BlockSpec(memory_space=pltpu.VMEM)],
        out_specs=pl.BlockSpec(memory_space=pltpu.SMEM),
        out_shape=jax.ShapeDtypeStruct((1,), jnp.int32),
        scratch_shapes=[
            pltpu.VMEM((depth, 1, slab), jnp.int32),
            pltpu.SemaphoreType.DMA((depth,)),
            pltpu.SemaphoreType.DMA((depth,)),
        ],
        compiler_params=pltpu.CompilerParams(collective_id=len(sizes) + 1, has_side_effects=True),
        name="size_class",
    )(shear_rows.reshape(1, slab))


def classes_of(slab):
    top = -(-slab * RIM // GROUP) * GROUP
    rough = {int(slab * f) // GROUP * GROUP for f in (3.5, 4, 4.5, 5.5)}
    return sorted({h for h in rough if h >= 2 * GROUP} | {top})


def per_device(volume, shear_rows, shear_cols, warp_cols, warp_rows):
    channels, slab, rows, cols = volume.shape
    depth = lax.axis_size("depth")
    n_rows = lax.axis_size("rows")

    scalars = (shear_rows, shear_cols, warp_cols)
    sizes = classes_of(slab)
    which = class_of(sizes, depth, shear_rows)[0]
    branches = [
        functools.partial(slab_stage, size, number + 1, depth, n_rows)
        for number, size in enumerate(sizes)
    ]
    turn = warp_rows.reshape(1, -1)
    return lax.switch(which, branches, volume, scalars, turn)


def solution(mesh):
    return jax.shard_map(
        per_device,
        mesh=mesh,
        in_specs=(P(None, "depth", "rows", None), P("depth"), P("depth"), P(), P("depth")),
        out_specs=P(None, "rows", "depth"),
        check_vma=False,
    )
```
